32 devices in a mesh: dp: 16 (over z, y, core), fsdp: 2 (over x).
Axes of the slice: x: 2, y: 2, z: 4, core: 2. Of those that a mesh axis runs over, the one named last changes fastest.
Arguments:
- tile_embeds: bfloat16 [2, 32, 256, 768], P(None, ('dp', 'fsdp')), may hold values from -6 to 6
- sentence_embeds: bfloat16 [2, 96, 64, 768], P(None, ('dp', 'fsdp')), may hold values from -6 to 6
- sentence_picture_map: int32 [2, 96], replicated, may hold values from 0 to 31, as said below
- picture_early_scaler: bfloat16 [768], P(('dp', 'fsdp')), may hold values from 0.5 to 1.5
- picture_early_shifter: bfloat16 [768], P(('dp', 'fsdp')), may hold values from -0.59765625 to 0.59765625
- picture_triplet_matrix: bfloat16 [768, 2304], P(('dp', 'fsdp')), may hold values from -0.375 to 0.375
- picture_mixer_projector: bfloat16 [768, 768], P(('dp', 'fsdp')), may hold values from -0.15625 to 0.15625
- picture_later_scaler: bfloat16 [768], P(('dp', 'fsdp')), may hold values from 0.5 to 1.5
- picture_later_shifter: bfloat16 [768], P(('dp', 'fsdp')), may hold values from -0.59765625 to 0.59765625
- picture_widen_matrix: bfloat16 [768, 3072], P(('dp', 'fsdp')), may hold values from -0.21875 to 0.21875
- picture_shrink_matrix: bfloat16 [3072, 768], P(('dp', 'fsdp')), may hold values from -0.109375 to 0.109375
- pregather_scaler: bfloat16 [768], P(('dp', 'fsdp')), may hold values from 0.5 to 1.5
- pregather_shifter: bfloat16 [768], P(('dp', 'fsdp')), may hold values from -0.59765625 to 0.59765625
- gather_probe_vectors: bfloat16 [768], P(('dp', 'fsdp')), may hold values from -5 to 5
- gather_lookup_matrix: bfloat16 [768, 1536], P(('dp', 'fsdp')), may hold values from -0.21875 to 0.21875
- gather_result_matrix: bfloat16 [768, 768], P(('dp', 'fsdp')), may hold values from -0.21875 to 0.21875
- wording_early_scaler: bfloat16 [768], P(('dp', 'fsdp')), may hold values from 0.5 to 1.5
- wording_early_shifter: bfloat16 [768], P(('dp', 'fsdp')), may hold values from -0.59765625 to 0.59765625
- wording_triplet_matrix: bfloat16 [768, 2304], P(('dp', 'fsdp')), may hold values from -0.375 to 0.375
- wording_mixer_projector: bfloat16 [768, 768], P(('dp', 'fsdp')), may hold values from -0.15625 to 0.15625
- wording_later_scaler: bfloat16 [768], P(('dp', 'fsdp')), may hold values from 0.5 to 1.5
- wording_later_shifter: bfloat16 [768], P(('dp', 'fsdp')), may hold values from -0.59765625 to 0.59765625
- wording_widen_matrix: bfloat16 [768, 3072], P(('dp', 'fsdp')), may hold values from -0.21875 to 0.21875
- wording_shrink_matrix: bfloat16 [3072, 768], P(('dp', 'fsdp')), may hold values from -0.109375 to 0.109375
- wording_closing_scaler: bfloat16 [768], P(('dp', 'fsdp')), may hold values from 0.5 to 1.5
- wording_closing_shifter: bfloat16 [768], P(('dp', 'fsdp')), may hold values from -0.59765625 to 0.59765625
- wording_readout_matrix: bfloat16 [768, 768], P(('dp', 'fsdp')), may hold values from -0.21875 to 0.21875
- sharpness_exponent: float32 [1], replicated, may hold values from 2 to 2.5
- match_score_offset: float32 [1], replicated, may hold values from -6 to -3
Outputs:
- image_embedding: float32 [2, 32, 768], P(None, ('dp', 'fsdp'))
- text_embedding: float32 [2, 96, 768], P(None, ('dp', 'fsdp'))
- penalty_amount: float32 [], replicated
- patches_grad: float32 [2, 32, 256, 768], P(None, ('dp', 'fsdp'))
- captions_grad: float32 [2, 96, 64, 768], P(None, ('dp', 'fsdp'))
- visual_gain_grad: float32 [768], P(('dp', 'fsdp'))
- visual_shift_grad: float32 [768], P(('dp', 'fsdp'))
- visual_triple_grad: float32 [768, 2304], P(('dp', 'fsdp'))
- visual_merge_grad: float32 [768, 768], P(('dp', 'fsdp'))
- visual_scale_grad: float32 [768], P(('dp', 'fsdp'))
- visual_offset_grad: float32 [768], P(('dp', 'fsdp'))
- visual_expand_grad: float32 [768, 3072], P(('dp', 'fsdp'))
- visual_reduce_grad: float32 [3072, 768], P(('dp', 'fsdp'))
- pooling_gain_grad: float32 [768], P(('dp', 'fsdp'))
- pooling_shift_grad: float32 [768], P(('dp', 'fsdp'))
- pooling_probe_grad: float32 [768], P(('dp', 'fsdp'))
- pooling_keyval_grad: float32 [768, 1536], P(('dp', 'fsdp'))
- pooling_output_grad: float32 [768, 768], P(('dp', 'fsdp'))
- textual_gain_grad: float32 [768], P(('dp', 'fsdp'))
- textual_shift_grad: float32 [768], P(('dp', 'fsdp'))
- textual_triple_grad: float32 [768, 2304], P(('dp', 'fsdp'))
- textual_merge_grad: float32 [768, 768], P(('dp', 'fsdp'))
- textual_scale_grad: float32 [768], P(('dp', 'fsdp'))
- textual_offset_grad: float32 [768], P(('dp', 'fsdp'))
- textual_expand_grad: float32 [768, 3072], P(('dp', 'fsdp'))
- textual_reduce_grad: float32 [3072, 768], P(('dp', 'fsdp'))
- closing_gain_grad: float32 [768], P(('dp', 'fsdp'))
- closing_shift_grad: float32 [768], P(('dp', 'fsdp'))
- textual_head_grad: float32 [768, 768], P(('dp', 'fsdp'))
- log_temperature_grad: float32 [1], replicated
- logit_bias_grad: float32 [1], replicated
The draws below stay inside these ranges and needn't reach their ends.
Inputs may be any that keep to these rules, and one draw needn't show every extreme that they name: `sentence_picture_map`: in each micro-batch every image is described by 2 to 5 captions: 4 images by 5, 8 by 4, 4 by 3 and the other half by 2; the captions stand in no order.
All inputs are finite; a program needn't handle non-finite values.
Results may differ from the reference program's by a relative error of at most 0.025.
Values may be sent and summed in bfloat16 or wider, within the bound.
No kernel may reach another device: no remote copies, remote signals or barrier semaphores. Data moves between devices by JAX's collectives and lax.ppermute only.
A program may use at most 320 MiB of HBM per device.

```python
import math
from functools import partial
import jax
import jax.numpy as jnp
from jax import lax

D = 768
HD = 64
FF = 3072
P_SIZE = 256
LT = 64
MB = 2
IMAGES = 32
CAPTIONS = 96


def draw_sentence_picture_map(key, part):
    rows_list = []
    for step_index in range(MB):
        sub_key = jax.random.fold_in(key, step_index)
        ranking = jax.random.permutation(jax.random.fold_in(sub_key, 1), IMAGES)
        counts = jnp.where(ranking < IMAGES // 8, 5, jnp.where(ranking < 3 * IMAGES // 8, 4, jnp.where(ranking < IMAGES // 2, 3, 2))).astype(jnp.int32)
        owners = jnp.repeat(jnp.arange(IMAGES, dtype=jnp.int32), counts, total_repeat_length=CAPTIONS)
        shuffle = jax.random.permutation(jax.random.fold_in(sub_key, 2), CAPTIONS)
        rows_list.append(owners[shuffle])
    return jnp.stack(rows_list).astype(jnp.int32)


def shard_levels(own_key, shape, split, low, largest):
    level = 1.0
    for dim, shards_of in split:
        draws = jax.random.uniform(jax.random.fold_in(jax.random.fold_in(own_key, 6), dim), (shards_of,), jnp.float32, low / len(split), largest / len(split))
        level = level * jnp.repeat(jnp.exp(draws), shape[dim] // shards_of).reshape((-1,) + (1,) * (len(shape) - 1 - dim))
    return level


def gaussian(own_key, shape, spread, limit, split=(), kind=jnp.bfloat16):
    entries = jax.random.normal(own_key, shape, jnp.float32) * spread
    if len(split) > 0:
        entries = shard_levels(own_key, shape, split, -0.22, 0.18) * entries
    return jnp.clip(entries, min=-limit, max=limit).astype(kind)


def setup_inputs(seed: int = 0) -> dict:
    key_list = jax.random.split(jax.random.key(seed), 30)
    tile_embeds = gaussian(key_list[0], (MB, IMAGES, P_SIZE, D), 1.0, 6.0, ((1, 32),))
    sentence_embeds = gaussian(key_list[1], (MB, CAPTIONS, LT, D), 1.0, 6.0, ((1, 32),))
    sentence_picture_map = draw_sentence_picture_map(jax.random.fold_in(key_list[29], 71), 0)
    picture_early_scaler = jnp.clip(1.0 + 0.1 * jax.random.normal(key_list[3], (D,), jnp.float32), 0.5, 1.5).astype(jnp.bfloat16)
    picture_early_shifter = gaussian(key_list[4], (D,), 0.15, 0.59765625, ((0, 32),))
    picture_triplet_matrix = gaussian(key_list[5], (D, 3 * D), (D // 3) ** -0.5, 0.375, ((0, 32),))
    picture_mixer_projector = gaussian(key_list[6], (D, D), (2 * D) ** -0.5, 0.15625, ((0, 32),))
    picture_later_scaler = jnp.clip(1.0 + 0.1 * jax.random.normal(key_list[7], (D,), jnp.float32), 0.5, 1.5).astype(jnp.bfloat16)
    picture_later_shifter = gaussian(key_list[8], (D,), 0.15, 0.59765625, ((0, 32),))
    picture_widen_matrix = gaussian(key_list[9], (D, FF), D ** -0.5, 0.21875, ((0, 32),))
    picture_shrink_matrix = gaussian(key_list[10], (FF, D), FF ** -0.5, 0.109375, ((0, 32),))
    pregather_scaler = jnp.clip(1.0 + 0.1 * jax.random.normal(key_list[11], (D,), jnp.float32), 0.5, 1.5).astype(jnp.bfloat16)
    pregather_shifter = gaussian(key_list[12], (D,), 0.15, 0.59765625, ((0, 32),))
    gather_probe_vectors = gaussian(key_list[13], (D,), 1.0, 5.0, ((0, 32),))
    gather_lookup_matrix = gaussian(key_list[14], (D, 2 * D), D ** -0.5, 0.21875, ((0, 32),))
    gather_result_matrix = gaussian(key_list[15], (D, D), D ** -0.5, 0.21875, ((0, 32),))
    wording_early_scaler = jnp.clip(1.0 + 0.1 * jax.random.normal(key_list[16], (D,), jnp.float32), 0.5, 1.5).astype(jnp.bfloat16)
    wording_early_shifter = gaussian(key_list[17], (D,), 0.15, 0.59765625, ((0, 32),))
    wording_triplet_matrix = gaussian(key_list[18], (D, 3 * D), (D // 3) ** -0.5, 0.375, ((0, 32),))
    wording_mixer_projector = gaussian(key_list[19], (D, D), (2 * D) ** -0.5, 0.15625, ((0, 32),))
    wording_later_scaler = jnp.clip(1.0 + 0.1 * jax.random.normal(key_list[20], (D,), jnp.float32), 0.5, 1.5).astype(jnp.bfloat16)
    wording_later_shifter = gaussian(key_list[21], (D,), 0.15, 0.59765625, ((0, 32),))
    wording_widen_matrix = gaussian(key_list[22], (D, FF), D ** -0.5, 0.21875, ((0, 32),))
    wording_shrink_matrix = gaussian(key_list[23], (FF, D), FF ** -0.5, 0.109375, ((0, 32),))
    wording_closing_scaler = jnp.clip(1.0 + 0.1 * jax.random.normal(key_list[24], (D,), jnp.float32), 0.5, 1.5).astype(jnp.bfloat16)
    wording_closing_shifter = gaussian(key_list[25], (D,), 0.15, 0.59765625, ((0, 32),))
    wording_readout_matrix = gaussian(key_list[26], (D, D), D ** -0.5, 0.21875, ((0, 32),))
    sharpness_exponent = jnp.clip(jax.random.uniform(key_list[27], (1,), jnp.float32, 2.0, 2.5), 2.0, 2.5)
    match_score_offset = jnp.clip(jax.random.uniform(key_list[28], (1,), jnp.float32, -6.0, -3.0), -6.0, -3.0)
    return {"tile_embeds": tile_embeds, "sentence_embeds": sentence_embeds, "sentence_picture_map": sentence_picture_map, "picture_early_scaler": picture_early_scaler, "picture_early_shifter": picture_early_shifter, "picture_triplet_matrix": picture_triplet_matrix, "picture_mixer_projector": picture_mixer_projector, "picture_later_scaler": picture_later_scaler, "picture_later_shifter": picture_later_shifter, "picture_widen_matrix": picture_widen_matrix, "picture_shrink_matrix": picture_shrink_matrix, "pregather_scaler": pregather_scaler, "pregather_shifter": pregather_shifter, "gather_probe_vectors": gather_probe_vectors, "gather_lookup_matrix": gather_lookup_matrix, "gather_result_matrix": gather_result_matrix, "wording_early_scaler": wording_early_scaler, "wording_early_shifter": wording_early_shifter, "wording_triplet_matrix": wording_triplet_matrix, "wording_mixer_projector": wording_mixer_projector, "wording_later_scaler": wording_later_scaler, "wording_later_shifter": wording_later_shifter, "wording_widen_matrix": wording_widen_matrix, "wording_shrink_matrix": wording_shrink_matrix, "wording_closing_scaler": wording_closing_scaler, "wording_closing_shifter": wording_closing_shifter, "wording_readout_matrix": wording_readout_matrix, "sharpness_exponent": sharpness_exponent, "match_score_offset": match_score_offset}


@jax.custom_vjp
def low(v):
    return lax.optimization_barrier(v.astype(jnp.bfloat16)).astype(jnp.float32)

@jax.custom_vjp
def low_back(v):
    return v

def low_keep(v):
    return (low(v), None)

def low_pass(kept, grad):
    return (grad,)

def back_keep(v):
    return (v, None)

def back_low(kept, grad):
    return (low(grad),)
low.defvjp(low_keep, low_pass)
low_back.defvjp(back_keep, back_low)
PRECISE = lax.Precision.HIGHEST
GELU_COEF = 0.7978845608028654
GELU_CUBE = 0.044715

def product(form, left, right):
    return jnp.einsum(form, left, right, precision=PRECISE)

def layer_norm(values, gain, shift):
    centred = values - lax.optimization_barrier(jnp.mean(values, axis=-1, keepdims=True))
    inverse = lax.rsqrt(lax.optimization_barrier(jnp.mean(centred * centred, axis=-1, keepdims=True)) + 1e-06)
    return centred * inverse * gain + shift

def gelu_tanh(values):
    return 0.5 * values * (1.0 + jnp.tanh(GELU_COEF * (values + GELU_CUBE * values * values * values)))

def unit_rows(embed):
    return embed * lax.rsqrt(lax.optimization_barrier(jnp.sum(embed * embed, axis=-1, keepdims=True)) + 1e-06)

def block(inputs, weights, causal):
    gain_a, shift_a, triple, merge, gain_b, shift_b, expand, shrink = weights
    row_count, seq_len, model_width = inputs.shape
    head_count = model_width // HD
    normed_a = low(layer_norm(inputs, gain_a, shift_a))
    triples = low(low_back(product('bsd,de->bse', normed_a, triple)))
    heads_view = triples.reshape(row_count, seq_len, 3, head_count, HD)
    scores = low_back(product('bqhd,bkhd->bhqk', heads_view[:, :, 0], heads_view[:, :, 1]) * HD ** (-0.5))
    if causal:
        allowed = jnp.tril(jnp.ones((seq_len, seq_len), dtype=bool))
        scores = jnp.where(allowed, scores, -1e+30)
    attn_probs = low(jax.nn.softmax(scores, axis=-1))
    mixed = product('bhqk,bkhd->bqhd', attn_probs, heads_view[:, :, 2]).reshape(row_count, seq_len, model_width)
    mixed = low(low_back(mixed))
    middle = inputs + low_back(product('bsd,de->bse', mixed, merge))
    normed_b = low(layer_norm(middle, gain_b, shift_b))
    upward = low_back(product('bsd,df->bsf', normed_b, expand))
    active = low(gelu_tanh(upward))
    return middle + low_back(product('bsf,fd->bsd', active, shrink))

def image_tower(picture_vectors, patch_group):
    hidden = block(patch_group, picture_vectors[:8], False)
    post_gain, post_shift, probe, keyval, pool_out = picture_vectors[8:]
    group_size, seq_len, model_width = hidden.shape
    head_count = model_width // HD
    normed = low(layer_norm(hidden, post_gain, post_shift))
    pairs = low(low_back(product('bsd,de->bse', normed, keyval)))
    pairs = pairs.reshape(group_size, seq_len, 2, head_count, HD)
    scores = low_back(product('hd,bkhd->bhk', probe.reshape(head_count, HD), pairs[:, :, 0]) * HD ** (-0.5))
    pool_probs = low(jax.nn.softmax(scores, axis=-1))
    pooled = product('bhk,bkhd->bhd', pool_probs, pairs[:, :, 1]).reshape(group_size, model_width)
    pooled = low(low_back(pooled))
    embed = low_back(product('bd,de->be', pooled, pool_out))
    return unit_rows(embed)

def text_tower(wording_vectors, caption_group):
    hidden = block(caption_group, wording_vectors[:8], True)
    final_gain, final_shift, head_matrix = wording_vectors[8:]
    last_row = low(layer_norm(hidden[:, -1], final_gain, final_shift))
    embed = low_back(product('bd,de->be', last_row, head_matrix))
    return unit_rows(embed)

def criterion_amount(patch_f, caption_f, picture_vectors, wording_vectors, log_temp, bias_value, sentence_picture_map):
    image_group = math.gcd(IMAGES, max(1, 4096 // P_SIZE))
    text_group = math.gcd(CAPTIONS, max(1, 4096 // LT))
    running = jnp.zeros((), jnp.float32)
    image_list = []
    text_list = []
    owners = jnp.arange(IMAGES, dtype=jnp.int32)
    for micro_step in range(MB):
        image_unit = lax.map(jax.checkpoint(partial(image_tower, picture_vectors)), patch_f[micro_step].reshape(IMAGES // image_group, image_group, P_SIZE, D))
        image_unit = image_unit.reshape(IMAGES, D)
        text_unit = lax.map(jax.checkpoint(partial(text_tower, wording_vectors)), caption_f[micro_step].reshape(CAPTIONS // text_group, text_group, LT, D))
        text_unit = text_unit.reshape(CAPTIONS, D)
        angular_match = low_back(product('id,jd->ij', low(image_unit), low(text_unit)))
        match_scores = jnp.exp(log_temp[0]) * angular_match + bias_value[0]
        signs = jnp.where(sentence_picture_map[micro_step][None, :] == owners[:, None], 1.0, -1.0)
        running = running + jnp.sum(jax.nn.softplus(-signs * match_scores))
        image_list.append(image_unit)
        text_list.append(text_unit)
    return (running, (jnp.stack(image_list), jnp.stack(text_list)))

def reference(tile_embeds, sentence_embeds, sentence_picture_map, picture_early_scaler, picture_early_shifter, picture_triplet_matrix, picture_mixer_projector, picture_later_scaler, picture_later_shifter, picture_widen_matrix, picture_shrink_matrix, pregather_scaler, pregather_shifter, gather_probe_vectors, gather_lookup_matrix, gather_result_matrix, wording_early_scaler, wording_early_shifter, wording_triplet_matrix, wording_mixer_projector, wording_later_scaler, wording_later_shifter, wording_widen_matrix, wording_shrink_matrix, wording_closing_scaler, wording_closing_shifter, wording_readout_matrix, sharpness_exponent, match_score_offset):
    picture_vectors = tuple((item.astype(jnp.float32) for item in (picture_early_scaler, picture_early_shifter, picture_triplet_matrix, picture_mixer_projector, picture_later_scaler, picture_later_shifter, picture_widen_matrix, picture_shrink_matrix, pregather_scaler, pregather_shifter, gather_probe_vectors, gather_lookup_matrix, gather_result_matrix)))
    wording_vectors = tuple((item.astype(jnp.float32) for item in (wording_early_scaler, wording_early_shifter, wording_triplet_matrix, wording_mixer_projector, wording_later_scaler, wording_later_shifter, wording_widen_matrix, wording_shrink_matrix, wording_closing_scaler, wording_closing_shifter, wording_readout_matrix)))
    overall_number, reverse_mode_rule, member_number = jax.vjp(partial(criterion_amount, sentence_picture_map=sentence_picture_map), tile_embeds.astype(jnp.float32), sentence_embeds.astype(jnp.float32), picture_vectors, wording_vectors, sharpness_exponent, match_score_offset, has_aux=True)
    tile_embeds_deriv, sentence_embeds_deriv, picture_deriv, wording_deriv, sharpness_deriv, offset_deriv = reverse_mode_rule(jnp.ones_like(overall_number))
    penalty_amount = overall_number / (MB * IMAGES)
    return (member_number[0], member_number[1], penalty_amount, tile_embeds_deriv, sentence_embeds_deriv, picture_deriv[0], picture_deriv[1], picture_deriv[2], picture_deriv[3], picture_deriv[4], picture_deriv[5], picture_deriv[6], picture_deriv[7], picture_deriv[8], picture_deriv[9], picture_deriv[10], picture_deriv[11], picture_deriv[12], wording_deriv[0], wording_deriv[1], wording_deriv[2], wording_deriv[3], wording_deriv[4], wording_deriv[5], wording_deriv[6], wording_deriv[7], wording_deriv[8], wording_deriv[9], wording_deriv[10], sharpness_deriv, offset_deriv)
```

```python
import functools

import jax
import jax.numpy as jnp
from jax import lax
from jax.experimental import pallas as pl
from jax.experimental.pallas import tpu as pltpu
from jax.sharding import PartitionSpec as P

HD = 64
AXES = ("dp", "fsdp")
GELU_COEF = 0.7978845608028654
GELU_CUBE = 0.044715
F32 = jnp.float32
LOW = jnp.bfloat16
SCALE = HD ** (-0.5)

BLOCKS = 15
CHAIN_BLOCKS = 5
VEC_ROWS = 8


def dot(left, right, left_dim, right_dim):
    return lax.dot_general(
        left, right, (((left_dim,), (right_dim,)), ((), ())), preferred_element_type=F32
    )


def normalize_rows(values):
    centred = values - jnp.mean(values, axis=-1, keepdims=True)
    inverse = lax.rsqrt(jnp.mean(centred * centred, axis=-1, keepdims=True) + 1e-06)
    return (centred * inverse, inverse)


def normalize_back(grad_hat, hat_rows, inverse):
    first = jnp.mean(grad_hat, axis=-1, keepdims=True)
    second = jnp.mean(grad_hat * hat_rows, axis=-1, keepdims=True)
    return inverse * (grad_hat - first - hat_rows * second)


def gelu_tanh(values):
    return (
        0.5 * values * (1.0 + jnp.tanh(GELU_COEF * (values + GELU_CUBE * values * values * values)))
    )


def gelu_slope(values):
    tanh_val = jnp.tanh(GELU_COEF * (values + GELU_CUBE * values * values * values))
    return 0.5 * (1.0 + tanh_val) + 0.5 * values * (1.0 - tanh_val * tanh_val) * GELU_COEF * (
        1.0 + 3.0 * GELU_CUBE * values * values
    )


def head_probs(allowed, query, key):
    scores = dot(query, key, 1, 1) * SCALE
    scores = jnp.where(allowed, scores, -1e30)
    row_exp = jnp.exp(scores - jnp.max(scores, axis=-1, keepdims=True))
    return row_exp * (1.0 / jnp.sum(row_exp, axis=-1, keepdims=True))


def allowed_pairs(side_ref, seq_len, group):
    row = lax.broadcasted_iota(jnp.int32, (seq_len, seq_len), 0)
    col = lax.broadcasted_iota(jnp.int32, (seq_len, seq_len), 1)
    causal = jnp.logical_and(row // group == col // group, row >= col)
    return jnp.logical_or(causal, side_ref[0] == 0)


def attend_kernel(group, side_ref, q_ref, k_ref, v_ref, out_ref):
    allowed = allowed_pairs(side_ref, q_ref.shape[0], group)
    parts = []
    for head in range(2):
        lanes = slice(head * HD, (head + 1) * HD)
        probs = head_probs(allowed, q_ref[:, lanes], k_ref[:, lanes]).astype(LOW)
        parts.append(dot(probs, v_ref[:, lanes], 1, 0))
    out_ref[...] = jnp.concatenate(parts, axis=1).astype(LOW)


def attend_back_kernel(group, width, side_ref, q_ref, k_ref, v_ref, grad_ref, out_ref):
    pair = pl.program_id(1)
    allowed = allowed_pairs(side_ref, q_ref.shape[0], group)
    parts = ([], [], [])
    for head in range(2):
        lanes = slice(head * HD, (head + 1) * HD)
        query, key, value = q_ref[:, lanes], k_ref[:, lanes], v_ref[:, lanes]
        grad = grad_ref[:, lanes]
        probs = head_probs(allowed, query, key)
        grad_probs = dot(grad, value, 1, 1)
        delta = jnp.sum(grad_probs * probs, axis=-1, keepdims=True)
        grad_scores = (probs * (grad_probs - delta)).astype(LOW)
        parts[0].append(dot(grad_scores, key, 1, 0) * SCALE)
        parts[1].append(dot(grad_scores, query, 0, 0) * SCALE)
        parts[2].append(dot(probs.astype(LOW), grad, 0, 0))
    for place in range(3):
        start = pl.multiple_of(place * width + pair * 2 * HD, 2 * HD)
        out_ref[:, pl.ds(start, 2 * HD)] = jnp.concatenate(parts[place], axis=1).astype(LOW)


def triple_specs(seq_len, pairs):
    return [
        pl.BlockSpec((seq_len, 2 * HD), lambda b, p, s, place=place: (b, place * pairs + p))
        for place in range(3)
    ]


def attend(side, triples, seq_len, group):
    rows, wide = triples.shape
    width = wide // 3
    pairs = width // (2 * HD)
    return pl.pallas_call(
        functools.partial(attend_kernel, group),
        out_shape=jax.ShapeDtypeStruct((rows, width), LOW),
        grid_spec=pltpu.PrefetchScalarGridSpec(
            num_scalar_prefetch=1,
            grid=(rows // seq_len, pairs),
            in_specs=triple_specs(seq_len, pairs),
            out_specs=pl.BlockSpec((seq_len, 2 * HD), lambda b, p, s: (b, p)),
        ),
        cost_estimate=pl.CostEstimate(
            flops=4 * rows * seq_len * width,
            bytes_accessed=8 * rows * width,
            transcendentals=rows * seq_len * width // HD,
        ),
        name="attend",
    )(side, triples, triples, triples)


def attend_back(side, triples, grad_mixed, seq_len, group):
    rows, wide = triples.shape
    width = wide // 3
    pairs = width // (2 * HD)
    return pl.pallas_call(
        functools.partial(attend_back_kernel, group, width),
        out_shape=jax.ShapeDtypeStruct((rows, wide), LOW),
        grid_spec=pltpu.PrefetchScalarGridSpec(
            num_scalar_prefetch=1,
            grid=(rows // seq_len, pairs),
            in_specs=triple_specs(seq_len, pairs)
            + [pl.BlockSpec((seq_len, 2 * HD), lambda b, p, s: (b, p))],
            out_specs=pl.BlockSpec((seq_len, wide), lambda b, p, s: (b, 0)),
        ),
        cost_estimate=pl.CostEstimate(
            flops=10 * rows * seq_len * width,
            bytes_accessed=14 * rows * width,
            transcendentals=rows * seq_len * width // HD,
        ),
        name="attend_back",
    )(side, triples, triples, triples, grad_mixed)


class Links:
    def __init__(self, count):
        self.count = count
        self.half = count // 2
        self.core = 2
        bits = [1 << place for place in range(self.half.bit_length() - 1)]
        outer = [bit for bit in bits if bit != self.core]
        third = max(1, len(outer) // 3)
        self.orders = [outer[place:] + outer[:place] for place in (0, third, 2 * third)]

    def swap(self, value, mask):
        return lax.ppermute(value, AXES, [(place, place ^ mask) for place in range(self.count)])


def gather_chain(links, order, start):
    held, masks = start[None], [0]
    for bit in order[:-1]:
        held = jnp.concatenate((held, links.swap(held, bit)), axis=0)
        masks = masks + [mask ^ bit for mask in masks]
    far = links.swap(held, order[-1])
    far_masks = [mask ^ order[-1] for mask in masks]
    pieces = [held, far, links.swap(held, links.core), links.swap(far, links.core)]
    other = [mask ^ links.core for mask in masks]
    far_other = [mask ^ links.core for mask in far_masks]
    return pieces, [masks, far_masks, other, far_other]


def unpack_chain(links, device, pieces, masks):
    low, side = device % links.half, device // links.half
    flat = [mask for group in masks for mask in group]
    place = [0] * links.half
    for slot, mask in enumerate(flat):
        place[mask] = slot
    slots = jnp.array(place, jnp.int32)[jnp.arange(links.half, dtype=jnp.int32) ^ low]
    whole = jnp.take(jnp.concatenate(pieces, axis=0), slots, axis=0)
    first = jnp.where(side == 0, whole[:, 0], whole[:, 1])
    second = jnp.where(side == 0, whole[:, 1], whole[:, 0])
    return jnp.concatenate((first, second), axis=0)


def pack_chain(links, device, order, whole):
    low, side = device % links.half, device // links.half
    masks = [0]
    for bit in order:
        masks = masks + [mask ^ bit for mask in masks]
    halves = whole.reshape((2, links.half) + whole.shape[1:])
    mine = jnp.where(side == 0, halves[0], halves[1])
    theirs = jnp.where(side == 0, halves[1], halves[0])
    both = jnp.stack((mine, theirs), axis=1)
    keep = jnp.take(both, jnp.array(masks, jnp.int32) ^ low, axis=0)
    send = jnp.take(both, jnp.array(masks, jnp.int32) ^ links.core ^ low, axis=0)
    return keep, send


def scatter_chain(links, order, keep, send):
    received = links.swap(send, links.core)
    total = None
    for bit in order[::-1]:
        near = keep.shape[0] // 2 if total is None else total.shape[0] // 2
        if total is None:
            far = (keep[near:].astype(F32) + received[near:].astype(F32)).astype(LOW)
            arrived = links.swap(far, bit)
            total = keep[:near].astype(F32) + received[:near].astype(F32) + arrived.astype(F32)
        else:
            arrived = links.swap(total[near:].astype(LOW), bit)
            total = total[:near] + arrived.astype(F32)
    return total[0]


def tower_block(matrices, vectors, rows, width):
    parts = []
    for item in matrices:
        if item is None:
            parts.append(jnp.zeros((rows, width), LOW))
        elif item.shape[1] == width:
            parts.append(item)
        else:
            parts.extend(jnp.split(item, item.shape[1] // width, axis=1))
    line = jnp.concatenate(vectors)
    line = jnp.pad(line, (0, width - line.shape[0]))
    parts.append(jnp.pad(line[None], ((0, VEC_ROWS - 1), (0, 0))))
    return jnp.concatenate(parts, axis=0)


def body(*args):
    tile_embeds, sentence_embeds, pairing = args[:3]
    visual_shards, textual_shards = args[3:16], args[16:27]
    sharpness_exponent, match_score_offset = args[27:]
    links = Links(lax.axis_size(AXES))
    count, half = links.count, links.half
    device = lax.axis_index(AXES)
    side, low = device // half, device % half
    on_images = side == 0
    side_word = jnp.reshape(side, (1,)).astype(jnp.int32)
    micro, images, seq_len, width = tile_embeds.shape
    captions, text_len = sentence_embeds.shape[1:3]
    own_rows = micro * images * seq_len
    text_rows = micro * captions * text_len
    row_shards = visual_shards[2].shape[0]

    (v_gain_a, v_shift_a, v_triple, v_merge, v_gain_b, v_shift_b, v_expand, v_shrink) = (
        visual_shards[:8]
    )
    pool_gain, pool_shift, probe, keyval, pool_out = visual_shards[8:]
    (t_gain_a, t_shift_a, t_triple, t_merge, t_gain_b, t_shift_b, t_expand, t_shrink) = (
        textual_shards[:8]
    )
    final_gain, final_shift, readout = textual_shards[8:]
    visual_block = tower_block(
        (v_triple, v_merge, v_expand, v_shrink, keyval, pool_out),
        (v_gain_a, v_shift_a, v_gain_b, v_shift_b, pool_gain, pool_shift, probe),
        row_shards,
        width,
    )
    textual_block = tower_block(
        (t_triple, t_merge, t_expand, t_shrink, None, None, readout),
        (t_gain_a, t_shift_a, t_gain_b, t_shift_b, final_gain, final_shift),
        row_shards,
        width,
    )
    own_block = jnp.where(on_images, visual_block, textual_block)
    their_block = links.swap(jnp.where(on_images, textual_block, visual_block), half)
    chain_rows = CHAIN_BLOCKS * row_shards
    gathered = []
    for chain, order in enumerate(links.orders):
        stop = (chain + 1) * chain_rows + (VEC_ROWS if chain == 2 else 0)
        rows = slice(chain * chain_rows, stop)
        pieces, masks = gather_chain(links, order, jnp.stack((own_block[rows], their_block[rows])))
        gathered.append(unpack_chain(links, device, pieces, masks))

    patch_rows = tile_embeds.reshape(own_rows, width)
    token_rows = jnp.pad(
        sentence_embeds.reshape(text_rows, width), ((0, own_rows - text_rows), (0, 0))
    )
    kept_rows = jnp.where(on_images, patch_rows, token_rows)
    moved_rows = links.swap(jnp.where(on_images, token_rows, patch_rows), half)

    def block_of(index):
        chain, place = divmod(index, CHAIN_BLOCKS)
        return gathered[chain][:, place * row_shards : (place + 1) * row_shards]

    def columns(first, many):
        return jnp.concatenate(
            [block_of(first + k).reshape(width, width) for k in range(many)], axis=1
        )

    triple, merge, expand = columns(0, 3), columns(3, 1), columns(4, 4)
    shrink = jnp.concatenate([block_of(8 + k) for k in range(4)], axis=1).reshape(4 * width, width)
    pool_keyval, head_matrix = columns(12, 2), columns(14, 1)
    lines = gathered[2][:, chain_rows, : 7 * row_shards].reshape(count, 7, row_shards)
    vectors = jnp.transpose(lines, (1, 0, 2)).reshape(7, width).astype(F32)
    gain_a, shift_a, gain_b, shift_b, gain_c, shift_c, probe_line = [vectors[k] for k in range(7)]

    inputs = jnp.concatenate((kept_rows, moved_rows), axis=0).astype(F32)
    hat_a, inverse_a = normalize_rows(inputs)
    normed_a = (hat_a * gain_a + shift_a).astype(LOW)
    triples = dot(normed_a, triple, 1, 0).astype(LOW)
    mixed = attend(side_word, triples, seq_len, text_len)
    middle = inputs + dot(mixed, merge, 1, 0)
    hat_b, inverse_b = normalize_rows(middle)
    normed_b = (hat_b * gain_b + shift_b).astype(LOW)
    upward = dot(normed_b, expand, 1, 0)
    active = gelu_tanh(upward).astype(LOW)
    hidden = middle + dot(active, shrink, 1, 0)

    total_rows = 2 * own_rows
    group_count = total_rows // seq_len
    caption_slots = total_rows // text_len
    heads = width // HD
    hat_c, inverse_c = normalize_rows(hidden)
    normed_c = (hat_c * gain_c + shift_c).astype(LOW)
    pairs = dot(normed_c, pool_keyval, 1, 0).astype(LOW)
    keys, values = pairs[:, :width], pairs[:, width:]
    lane = lax.broadcasted_iota(jnp.int32, (width, 128), 0) // HD
    spread = lane == lax.broadcasted_iota(jnp.int32, (width, 128), 1)
    probe_map = jnp.where(spread, probe_line[:, None], 0.0).astype(LOW)
    spread_low = spread.astype(LOW)
    scores = (dot(keys, probe_map, 1, 0) * SCALE).reshape(group_count, seq_len, 128)
    row_exp = jnp.exp(scores - jnp.max(scores, axis=1, keepdims=True))
    pool_full = row_exp / jnp.sum(row_exp, axis=1, keepdims=True)
    pool_probs = pool_full.astype(LOW).reshape(total_rows, 128)
    probs_wide = dot(pool_probs, spread_low, 1, 1)
    pooled = jnp.sum((probs_wide * values).reshape(group_count, seq_len, width), axis=1)
    pooled = jnp.pad(pooled.astype(LOW), ((0, caption_slots - group_count), (0, 0)))
    last_rows = normed_c.reshape(caption_slots, text_len, width)[:, -1]
    head_in = jnp.where(on_images, pooled, last_rows)
    raw = dot(head_in, head_matrix, 1, 0)
    length_inverse = lax.rsqrt(jnp.sum(raw * raw, axis=-1, keepdims=True) + 1e-06)
    unit = raw * length_inverse

    their_unit = links.swap(unit, half)
    image_units = jnp.where(on_images, unit, their_unit)[:group_count]
    text_units = jnp.where(on_images, their_unit, unit)
    own_texts = micro * captions
    caption_half = caption_slots // 2
    text_units = jnp.concatenate(
        (text_units[:own_texts], text_units[caption_half : caption_half + own_texts]), axis=0
    )
    held = jnp.concatenate((image_units, text_units), axis=0).astype(LOW)[None]
    masks = [0]
    for bit in links.orders[0] + [links.core]:
        held = jnp.concatenate((held, links.swap(held, bit)), axis=0)
        masks = masks + [mask ^ bit for mask in masks]
    slot_device = jnp.array(masks, jnp.int32) ^ low
    image_side = jnp.arange(2, dtype=jnp.int32)
    image_device = image_side[None, :] * half + slot_device[:, None]
    text_device = (1 - image_side)[None, :] * half + slot_device[:, None]
    steps = jnp.arange(micro, dtype=jnp.int32)[None, None, :, None]
    all_images, all_captions = count * images, count * captions
    image_row = (steps * count + image_device[:, :, None, None]) * images + jnp.arange(images)
    text_row = (steps * count + text_device[:, :, None, None]) * captions + jnp.arange(captions)
    image_row, text_row = image_row.reshape(-1), text_row.reshape(-1)
    held_images = held[:, :group_count].reshape(-1, width)
    held_texts = held[:, group_count:].reshape(-1, width)
    image_pick = jnp.arange(micro * all_images)[:, None] == image_row[None, :]
    text_pick = jnp.arange(micro * all_captions)[:, None] == text_row[None, :]
    images_low = dot(image_pick.astype(LOW), held_images, 1, 0).astype(LOW)
    texts_low = dot(text_pick.astype(LOW), held_texts, 1, 0).astype(LOW)

    sharpness_factor = jnp.exp(sharpness_exponent[0])
    cosine = dot(images_low, texts_low, 1, 1)
    image_at = jnp.arange(micro * all_images)
    text_at = jnp.arange(micro * all_captions)
    together = (image_at // all_images)[:, None] == (text_at // all_captions)[None, :]
    matched = pairing.reshape(-1)[None, :] == (image_at % all_images)[:, None]
    signs = jnp.where(matched, 1.0, -1.0)
    logits = sharpness_factor * cosine + match_score_offset[0]
    objective = jnp.sum(jnp.where(together, jax.nn.softplus(-signs * logits), 0.0))
    grad_logits = jnp.where(together, -signs * jax.nn.sigmoid(-signs * logits), 0.0)
    sharpness_grad = jnp.sum(grad_logits * cosine) * sharpness_factor
    offset_grad = jnp.sum(grad_logits)
    grad_cosine = (sharpness_factor * grad_logits).astype(LOW)
    own_images = jnp.pad(image_row[:group_count], (0, caption_slots - group_count), constant_values=-1)
    own_captions = text_row[: 2 * own_texts]
    gap = jnp.full((caption_half - own_texts,), -1, jnp.int32)
    own_captions = jnp.concatenate((own_captions[:own_texts], gap, own_captions[own_texts:], gap))
    pick_images = (own_images[:, None] == image_at[None, :]).astype(LOW)
    pick_texts = (own_captions[:, None] == text_at[None, :]).astype(LOW)
    from_texts = dot(dot(pick_images, grad_cosine, 1, 0).astype(LOW), texts_low, 1, 0)
    from_images = dot(dot(pick_texts, grad_cosine, 1, 1).astype(LOW), images_low, 1, 0)
    grad_unit = jnp.where(on_images, from_texts, from_images)

    grad_raw = length_inverse * (grad_unit - unit * jnp.sum(grad_unit * unit, axis=-1, keepdims=True))
    grad_raw = grad_raw.astype(LOW)
    grad_head = dot(head_in, grad_raw, 0, 0).astype(LOW)
    grad_head_in = dot(grad_raw, head_matrix, 1, 1)
    grad_pooled = grad_head_in[:group_count].astype(LOW)
    pooled_wide = jnp.broadcast_to(grad_pooled[:, None], (group_count, seq_len, width))
    pooled_wide = pooled_wide.reshape(total_rows, width)
    grad_values = probs_wide * pooled_wide
    pooled_map = jnp.where(spread[None], grad_pooled[:, :, None], 0.0).astype(LOW)
    grad_probs = lax.dot_general(
        values.reshape(group_count, seq_len, width),
        pooled_map,
        (((2,), (1,)), ((0,), (0,))),
        preferred_element_type=F32,
    )
    delta = jnp.sum(grad_probs * pool_full, axis=1, keepdims=True)
    grad_scores = (pool_full * (grad_probs - delta)).astype(LOW).reshape(total_rows, 128)
    grad_keys = dot(grad_scores, probe_map, 1, 1) * SCALE
    grad_probe = jnp.sum(jnp.where(spread, dot(keys, grad_scores, 0, 0), 0.0), axis=1) * SCALE
    grad_pairs = jnp.concatenate((grad_keys.astype(LOW), grad_values.astype(LOW)), axis=1)
    grad_keyval = dot(normed_c, grad_pairs, 0, 0).astype(LOW)
    pool_side = dot(grad_pairs, pool_keyval, 1, 1)
    text_side = jnp.pad(grad_head_in[:, None], ((0, 0), (text_len - 1, 0), (0, 0)))
    grad_normed_c = jnp.where(on_images, pool_side, text_side.reshape(total_rows, width))
    grad_gain_c = jnp.sum(grad_normed_c * hat_c, axis=0)
    grad_shift_c = jnp.sum(grad_normed_c, axis=0)
    grad_hidden = normalize_back(grad_normed_c * gain_c, hat_c, inverse_c)

    grad_low = grad_hidden.astype(LOW)
    grad_shrink = dot(active, grad_low, 0, 0).astype(LOW)
    grad_up = (dot(grad_low, shrink, 1, 1) * gelu_slope(upward)).astype(LOW)
    grad_expand = dot(normed_b, grad_up, 0, 0).astype(LOW)
    grad_normed_b = dot(grad_up, expand, 1, 1)
    grad_gain_b = jnp.sum(grad_normed_b * hat_b, axis=0)
    grad_shift_b = jnp.sum(grad_normed_b, axis=0)
    grad_middle = grad_hidden + normalize_back(grad_normed_b * gain_b, hat_b, inverse_b)
    grad_branch = grad_middle.astype(LOW)
    grad_merge = dot(mixed, grad_branch, 0, 0).astype(LOW)
    grad_mixed = dot(grad_branch, merge, 1, 1).astype(LOW)
    grad_triples = attend_back(side_word, triples, grad_mixed, seq_len, text_len)
    grad_triple = dot(normed_a, grad_triples, 0, 0).astype(LOW)
    grad_normed_a = dot(grad_triples, triple, 1, 1)
    grad_gain_a = jnp.sum(grad_normed_a * hat_a, axis=0)
    grad_shift_a = jnp.sum(grad_normed_a, axis=0)
    grad_inputs = grad_middle + normalize_back(grad_normed_a * gain_a, hat_a, inverse_a)

    def rows_of(grad):
        return [
            item.reshape(count, row_shards, width)
            for item in jnp.split(grad, grad.shape[1] // width, axis=1)
        ]

    shrink_rows = grad_shrink.reshape(count, 4 * row_shards, width)
    grad_lines = jnp.stack(
        (grad_gain_a, grad_shift_a, grad_gain_b, grad_shift_b, grad_gain_c, grad_shift_c, grad_probe)
    )
    grad_lines = jnp.transpose(grad_lines.reshape(7, count, row_shards), (1, 0, 2))
    grad_lines = grad_lines.reshape(count, 1, 7 * row_shards).astype(LOW)
    grad_lines = jnp.pad(grad_lines, ((0, 0), (0, VEC_ROWS - 1), (0, width - 7 * row_shards)))
    whole = jnp.concatenate(
        rows_of(grad_triple)
        + rows_of(grad_merge)
        + rows_of(grad_expand)
        + [shrink_rows]
        + rows_of(grad_keyval)
        + rows_of(grad_head)
        + [grad_lines],
        axis=1,
    )
    summed = []
    for chain, order in enumerate(links.orders):
        stop = (chain + 1) * chain_rows + (VEC_ROWS if chain == 2 else 0)
        keep, send = pack_chain(links, device, order, whole[:, chain * chain_rows : stop])
        summed.append(scatter_chain(links, order, keep, send))
    summed = jnp.concatenate(summed, axis=1)
    crossed = links.swap(summed[1].astype(LOW), half).astype(F32)
    visual_sum = jnp.where(on_images, summed[0], crossed)
    textual_sum = jnp.where(on_images, crossed, summed[0])

    def outputs_of(total, names):
        def cols(first, many):
            return jnp.concatenate(
                [total[(first + k) * row_shards : (first + k + 1) * row_shards] for k in range(many)],
                axis=1,
            )

        line = total[BLOCKS * row_shards]
        vec = [line[k * row_shards : (k + 1) * row_shards] for k in range(7)]
        layer = (
            vec[0],
            vec[1],
            cols(0, 3),
            cols(3, 1),
            vec[2],
            vec[3],
            cols(4, 4),
            total[8 * row_shards : 12 * row_shards],
        )
        if names == 0:
            return layer + (vec[4], vec[5], vec[6], cols(12, 2), cols(14, 1))
        return layer + (vec[4], vec[5], cols(14, 1))

    returned = links.swap(grad_inputs[own_rows:].astype(LOW), half).astype(F32)
    kept = grad_inputs[:own_rows]
    patches_grad = jnp.where(on_images, kept, returned).reshape(tile_embeds.shape)
    captions_grad = jnp.where(on_images, returned[:text_rows], kept[:text_rows])
    own_group = group_count // 2
    image_embedding = jnp.where(on_images, unit[:own_group], their_unit[own_group:group_count])
    text_embedding = jnp.where(
        on_images, their_unit[caption_half : caption_half + own_texts], unit[:own_texts]
    )
    return (
        image_embedding.reshape(micro, images, width),
        text_embedding.reshape(micro, captions, width),
        objective / (micro * all_images),
        patches_grad,
        captions_grad.reshape(sentence_embeds.shape),
        *outputs_of(visual_sum, 0),
        *outputs_of(textual_sum, 1),
        jnp.reshape(sharpness_grad, (1,)),
        jnp.reshape(offset_grad, (1,)),
    )


def solution(mesh):
    row, matrix, batch, rest = P(AXES), P(AXES, None), P(None, AXES, None, None), P()
    layer = (row, row, matrix, matrix, row, row, matrix, matrix)
    visual = layer + (row, row, row, matrix, matrix)
    textual = layer + (row, row, matrix)
    in_specs = (batch, batch, rest) + visual + textual + (rest, rest)
    embed = P(None, AXES, None)
    out_specs = (embed, embed, rest, batch, batch) + visual + textual + (rest, rest)
    return jax.shard_map(body, mesh=mesh, in_specs=in_specs, out_specs=out_specs, check_vma=False)
```

```python
import functools

import jax
import jax.numpy as jnp
import numpy as np
from jax import lax
from jax.experimental import pallas as pl
from jax.experimental.pallas import tpu as pltpu
from jax.sharding import PartitionSpec as P

HD = 64
AXES = ("dp", "fsdp")
GELU_COEF = 0.7978845608028654
GELU_CUBE = 0.044715
F32 = jnp.float32
LOW = jnp.bfloat16
SCALE = HD ** (-0.5)

LANES = 128
CHAINS = 3
GATHER_GROUPS = (
    (("triple", 3), ("merge", 1), ("line", 0)),
    (("expand", 4), ("keyval", 2), ("head", 1), ("shrink", 4)),
)
SCATTER_GROUPS = (
    (("head", 1), ("keyval", 2), ("shrink", 4)),
    (("expand", 4), ("merge", 1)),
    (("triple", 3), ("line", 0)),
)
IMAGE_ROWS = 8


def dot(left, right, left_dim, right_dim):
    return lax.dot_general(
        left, right, (((left_dim,), (right_dim,)), ((), ())), preferred_element_type=F32
    )


def normalize_rows(values):
    centred = values - jnp.mean(values, axis=-1, keepdims=True)
    inverse = lax.rsqrt(jnp.mean(centred * centred, axis=-1, keepdims=True) + 1e-06)
    return (centred * inverse, inverse)


def normalize_back(grad_hat, hat_rows, inverse):
    first = jnp.mean(grad_hat, axis=-1, keepdims=True)
    second = jnp.mean(grad_hat * hat_rows, axis=-1, keepdims=True)
    return inverse * (grad_hat - first - hat_rows * second)


def gelu_tanh(values):
    return (
        0.5 * values * (1.0 + jnp.tanh(GELU_COEF * (values + GELU_CUBE * values * values * values)))
    )


def gelu_slope(values):
    tanh_val = jnp.tanh(GELU_COEF * (values + GELU_CUBE * values * values * values))
    return 0.5 * (1.0 + tanh_val) + 0.5 * values * (1.0 - tanh_val * tanh_val) * GELU_COEF * (
        1.0 + 3.0 * GELU_CUBE * values * values
    )


def pair_bias(side_ref, seq_len, group):
    key = lax.broadcasted_iota(jnp.int32, (seq_len, seq_len), 0)
    query = lax.broadcasted_iota(jnp.int32, (seq_len, seq_len), 1)
    seen = jnp.logical_and(key // group == query // group, query >= key)
    seen = jnp.logical_or(seen, side_ref[0] == 0)
    return jnp.where(seen, 0.0, -1e30)

def head_lanes(shape):
    lane = lax.broadcasted_iota(jnp.int32, shape, 1)
    return (lane < HD, lane >= HD)

def head_probs(key, query_part, bias):
    scores = dot(key, query_part, 1, 1) + bias
    row_exp = jnp.exp(scores - jnp.max(scores, axis=0, keepdims=True))
    return row_exp * (1.0 / jnp.sum(row_exp, axis=0, keepdims=True))

def attend_kernel(group, side_ref, q_ref, k_ref, v_ref, out_ref, bias_ref):
    @pl.when(pl.program_id(0) == 0)
    def _():
        bias_ref[...] = pair_bias(side_ref, q_ref.shape[0], group)
    bias = bias_ref[...]
    pairs = q_ref.shape[1] // (2 * HD)
    def scores_of(pair):
        lanes = slice(pair * 2 * HD, (pair + 1) * 2 * HD)
        query, key = q_ref[:, lanes] * jnp.asarray(SCALE, LOW), k_ref[:, lanes]
        zero = jnp.zeros_like(query)
        return [dot(key, jnp.where(mine, query, zero), 1, 1) for mine in head_lanes(query.shape)]
    def finish(pair, scores):
        lanes = slice(pair * 2 * HD, (pair + 1) * 2 * HD)
        value_t = v_ref[:, lanes].T
        parts = []
        for head in range(2):
            masked = scores[head] + bias
            row_exp = jnp.exp(masked - jnp.max(masked, axis=0, keepdims=True))
            inverse = 1.0 / jnp.sum(row_exp, axis=0, keepdims=True)
            part = dot(value_t[head * HD : (head + 1) * HD], row_exp.astype(LOW), 1, 0)
            parts.append(part * inverse)
        out_ref[:, lanes] = jnp.concatenate(parts, axis=0).T.astype(LOW)
    for pair in range(pairs):
        finish(pair, scores_of(pair))

def attend_back_kernel(group, width, side_ref, q_ref, k_ref, v_ref, grad_ref, out_ref, bias_ref):
    @pl.when(pl.program_id(0) == 0)
    def _():
        bias_ref[...] = pair_bias(side_ref, q_ref.shape[0], group)
    bias = bias_ref[...]
    for pair in range(width // (2 * HD)):
        lanes = slice(pair * 2 * HD, (pair + 1) * 2 * HD)
        query, key, value = q_ref[:, lanes] * jnp.asarray(SCALE, LOW), k_ref[:, lanes], v_ref[:, lanes]
        grad = grad_ref[:, lanes]
        key_t = key.T
        zero = jnp.zeros_like(query)
        sides = head_lanes(query.shape)
        grad_q, grad_k, grad_v = [], [], []
        for head, mine in enumerate(sides):
            probs = head_probs(key, jnp.where(mine, query, zero), bias)
            grad_probs = dot(value, jnp.where(mine, grad, zero), 1, 1)
            delta = jnp.sum(grad_probs * probs, axis=0, keepdims=True)
            grad_scores = (probs * (grad_probs - delta)).astype(LOW)
            grad_q.append(dot(key_t[head * HD : (head + 1) * HD], grad_scores, 1, 0))
            grad_k.append(dot(grad_scores, query, 1, 0))
            grad_v.append(dot(probs.astype(LOW), grad, 1, 0))
        parts = (
            jnp.concatenate(grad_q, axis=0).T * SCALE,
            jnp.where(sides[0], grad_k[0], grad_k[1]),
            jnp.where(sides[0], grad_v[0], grad_v[1]),
        )
        for place, part in enumerate(parts):
            start = place * width + pair * 2 * HD
            out_ref[:, start : start + 2 * HD] = part.astype(LOW)

def triple_specs(seq_len, width):
    return [pl.BlockSpec((seq_len, width), lambda b, s, place=place: (b, place)) for place in range(3)]


def attend(side, triples, seq_len, group):
    rows, wide = triples.shape
    width = wide // 3
    return pl.pallas_call(
        functools.partial(attend_kernel, group),
        out_shape=jax.ShapeDtypeStruct((rows, width), LOW),
        grid_spec=pltpu.PrefetchScalarGridSpec(
            num_scalar_prefetch=1,
            grid=(rows // seq_len,),
            in_specs=triple_specs(seq_len, width),
            out_specs=pl.BlockSpec((seq_len, width), lambda b, s: (b, 0)),
            scratch_shapes=[pltpu.VMEM((seq_len, seq_len), F32)],
        ),
        cost_estimate=pl.CostEstimate(
            flops=4 * rows * seq_len * width,
            bytes_accessed=8 * rows * width,
            transcendentals=rows * seq_len * width // HD,
        ),
        name="attend",
    )(side, triples, triples, triples)


def attend_back(side, triples, grad_mixed, first, seq_len, group):
    rows, wide = triples.shape
    width = wide // 3
    return pl.pallas_call(
        functools.partial(attend_back_kernel, group, width),
        out_shape=jax.ShapeDtypeStruct((rows, wide), LOW),
        grid_spec=pltpu.PrefetchScalarGridSpec(
            num_scalar_prefetch=1,
            grid=(rows // seq_len,),
            in_specs=triple_specs(seq_len, width)
            + [pl.BlockSpec((seq_len, width), lambda b, s: (b + first, 0))],
            out_specs=pl.BlockSpec((seq_len, wide), lambda b, s: (b, 0)),
            scratch_shapes=[pltpu.VMEM((seq_len, seq_len), F32)],
        ),
        cost_estimate=pl.CostEstimate(
            flops=10 * rows * seq_len * width,
            bytes_accessed=14 * rows * width,
            transcendentals=rows * seq_len * width // HD,
        ),
        name="attend_back",
    )(side, triples, triples, triples, grad_mixed)


class Segment:
    def __init__(self, name, quarter, weight_col, chain, chain_col, cols):
        self.name, self.quarter, self.weight_col = name, quarter, weight_col
        self.chain, self.chain_col, self.cols = chain, chain_col, cols


class Group:
    def __init__(self, parts, width):
        self.names = [name for name, _ in parts]
        self.cols = {name: max(many * width, LANES) for name, many in parts}
        total = sum(self.cols.values())
        tiles = total // LANES
        cuts = [tiles * chain // CHAINS * LANES for chain in range(CHAINS + 1)]
        self.total = total
        self.bounds = list(zip(cuts[:-1], cuts[1:]))
        self.chain_cols = [stop - start for start, stop in self.bounds]
        self.segments, self.places = [], []
        at = 0
        for name, _ in parts:
            quarters = range(4) if name == "shrink" else (None,)
            cols = self.cols[name] // len(quarters)
            for quarter in quarters:
                self.places.append((name, quarter, at, cols))
                for chain, (start, stop) in enumerate(self.bounds):
                    low, high = max(at, start), min(at + cols, stop)
                    if low < high:
                        self.segments.append(
                            Segment(name, quarter, low - at, chain, low - start, high - low)
                        )
                at += cols

    def shape(self, name, count, rows):
        if name == "shrink":
            return (count, 4, rows, self.cols[name] // 4)
        return (count, rows, self.cols[name])


def window(ref, lead, quarter, col, cols):
    lead = lead if quarter is None else lead + (quarter,)
    return ref.at[lead + (slice(None), pl.ds(col, cols))]


def wait_whole(refs, sems):
    for place, ref in enumerate(refs):
        pltpu.make_async_copy(ref, ref, sems.at[place]).wait()


def block_call(kernel, operands, outs, name):
    anywhere = pl.BlockSpec(memory_space=pl.ANY)
    size = sum(2 * out.size * out.dtype.itemsize for out in outs)
    return pl.pallas_call(
        kernel,
        out_shape=outs,
        grid_spec=pltpu.PrefetchScalarGridSpec(
            num_scalar_prefetch=1,
            grid=(1,),
            in_specs=[anywhere] * (len(operands) - 1),
            out_specs=[pl.BlockSpec(memory_space=pltpu.VMEM)] * len(outs),
            scratch_shapes=[pltpu.SemaphoreType.DMA((len(outs),))],
        ),
        cost_estimate=pl.CostEstimate(flops=0, bytes_accessed=size, transcendentals=0),
        name=name,
    )(*operands)


def collect_kernel(groups, towers, side_ref, *refs):
    tower_refs = (refs[: len(towers[0])], refs[len(towers[0]) : len(towers[0]) + len(towers[1])])
    outs, sems = refs[len(towers[0]) + len(towers[1]) : -1], refs[-1]

    def fill(kept):
        for index, group in enumerate(groups):
            base = index * (CHAINS + 1)
            sources = dict(zip(towers[kept], tower_refs[kept]))
            for part in group.segments:
                if part.name in sources:
                    source = sources[part.name]
                    rows = outs[base].shape[0]
                    first = 0 if part.quarter is None else part.quarter * rows
                    pltpu.make_async_copy(
                        source.at[pl.ds(first, rows), pl.ds(part.weight_col, part.cols)],
                        outs[base + part.chain].at[:, pl.ds(part.chain_col, part.cols)],
                        sems.at[base + part.chain],
                    ).start()
            sources = dict(zip(towers[1 - kept], tower_refs[1 - kept]))
            for name, quarter, at, cols in group.places:
                if name in sources:
                    source = sources[name]
                    rows = outs[base].shape[0]
                    first = 0 if quarter is None else quarter * rows
                    pltpu.make_async_copy(
                        source.at[pl.ds(first, rows), :],
                        outs[base + CHAINS].at[:, pl.ds(at, cols)],
                        sems.at[base + CHAINS],
                    ).start()

    pl.when(side_ref[0] == 0)(lambda: fill(0))
    pl.when(side_ref[0] != 0)(lambda: fill(1))
    wait_whole(outs, sems)


def collect(side_word, groups, visual, textual, rows):
    outs = []
    for group in groups:
        outs += [jax.ShapeDtypeStruct((rows, cols), LOW) for cols in group.chain_cols]
        outs.append(jax.ShapeDtypeStruct((rows, group.total), LOW))
    if rows % 8 == 0:
        towers = (tuple(visual), tuple(textual))
        operands = (side_word,) + tuple(visual.values()) + tuple(textual.values())
        kernel = functools.partial(collect_kernel, groups, towers)
        flat = block_call(kernel, operands, outs, "collect")
    else:
        flat = []
        for group in groups:
            blocks = []
            for tower in (visual, textual):
                parts = []
                for name, quarter, _, cols in group.places:
                    first = 0 if quarter is None else quarter * rows
                    parts.append(tower[name][first : first + rows])
                blocks.append(jnp.concatenate(parts, axis=1))
            on_images = side_word[0] == 0
            mine = jnp.where(on_images, blocks[0], blocks[1])
            flat += [mine[:, start:stop] for start, stop in group.bounds]
            flat.append(jnp.where(on_images, blocks[1], blocks[0]))
    size = CHAINS + 1
    return [flat[k * size : (k + 1) * size] for k in range(len(groups))]


def spread_kernel(group, sizes, table_ref, *refs):
    pieces = refs[: sum(len(each) for each in sizes)]
    outs, sems = refs[len(pieces) : -1], refs[-1]
    place = {name: k for k, name in enumerate(group.names)}
    base, at = 0, 0
    for chain, each in enumerate(sizes):
        parts = [part for part in group.segments if part.chain == chain]
        for size in each:
            piece = pieces[at]
            at += 1

            def step(slot, carry, piece=piece, base=base, parts=parts):
                for j in range(2):
                    owner = table_ref[base + 2 * slot + j]
                    for part in parts:
                        target = place[part.name]
                        pltpu.make_async_copy(
                            window(piece, (slot, j), None, part.chain_col, part.cols),
                            window(outs[target], (owner,), part.quarter, part.weight_col, part.cols),
                            sems.at[target],
                        ).start()
                return carry

            lax.fori_loop(0, size, step, 0)
            base += 2 * size
    wait_whole(outs, sems)


def pack_kernel(group, slots, table_ref, *refs):
    grads, outs, sems = refs[: len(group.names)], refs[len(group.names) : -1], refs[-1]
    place = {name: k for k, name in enumerate(group.names)}
    for chain in range(CHAINS):
        parts = [part for part in group.segments if part.chain == chain]
        for which in range(2):
            base = (2 * chain + which) * 2 * slots
            target = 2 * chain + which

            def step(slot, carry, base=base, parts=parts, target=target):
                for j in range(2):
                    owner = table_ref[base + 2 * slot + j]
                    for part in parts:
                        source = grads[place[part.name]]
                        pltpu.make_async_copy(
                            window(source, (owner,), part.quarter, part.weight_col, part.cols),
                            window(outs[target], (slot, j), None, part.chain_col, part.cols),
                            sems.at[target],
                        ).start()
                return carry

            lax.fori_loop(0, slots, step, 0)
    wait_whole(outs, sems)


class Links:
    def __init__(self, count, device):
        self.count = count
        self.half = count // 2
        self.core = 2
        self.device = device
        self.low, self.side = device % self.half, device // self.half
        bits = [1 << place for place in range(self.half.bit_length() - 1)]
        outer = [bit for bit in bits if bit != self.core]
        third = max(1, len(outer) // 3)
        self.orders = [outer[place:] + outer[:place] for place in (0, third, 2 * third)]

    def swap(self, value, mask):
        return lax.ppermute(value, AXES, [(place, place ^ mask) for place in range(self.count)])

    def owners(self, masks):
        low = jnp.array(masks, jnp.int32) ^ self.low
        sides = jnp.stack((self.side, 1 - self.side)).astype(jnp.int32)
        return low[:, None] + sides[None, :] * self.half


def chain_masks(order):
    masks = [0]
    for bit in order:
        masks = masks + [mask ^ bit for mask in masks]
    return masks


def gather_chain(links, order, start):
    held = start[None]
    for bit in order[:-1]:
        held = jnp.concatenate((held, links.swap(held, bit)), axis=0)
    far = links.swap(held, order[-1])
    pieces = [held, far, links.swap(held, links.core), links.swap(far, links.core)]
    masks = chain_masks(order)
    return pieces, masks + [mask ^ links.core for mask in masks]


def gather_pieces(links, group, kept, arrived):
    return [
        gather_chain(links, order, jnp.stack((kept[chain], arrived[:, start:stop])))
        for chain, (order, (start, stop)) in enumerate(zip(links.orders, group.bounds))
    ]


def place_pieces(links, group, chains, rows):
    pieces = [got for got, _ in chains]
    sizes = [[piece.shape[0] for piece in got] for got in pieces]
    tables = [links.owners(masks) for _, masks in chains]
    shapes = [group.shape(name, links.count, rows) for name in group.names]
    if rows % 8 == 0:
        operands = (jnp.stack(tables).reshape(-1),) + tuple(p for got in pieces for p in got)
        outs = [jax.ShapeDtypeStruct(shape, LOW) for shape in shapes]
        kernel = functools.partial(spread_kernel, group, sizes)
        whole = block_call(kernel, operands, outs, "spread")
    else:
        columns = []
        for got, table in zip(pieces, tables):
            order = jnp.argsort(table.reshape(-1))
            every = jnp.concatenate(got, axis=0)
            columns.append(jnp.take(every.reshape((-1,) + every.shape[2:]), order, axis=0))
        every = jnp.concatenate(columns, axis=2)
        whole, at = [], 0
        for name in group.names:
            cols = group.cols[name]
            block = every[:, :, at : at + cols]
            if name == "shrink":
                block = block.reshape(links.count, rows, 4, cols // 4).transpose(0, 2, 1, 3)
            whole.append(block)
            at += cols
    result = {}
    for name, block in zip(group.names, whole):
        result[name] = block if name == "line" else block.reshape(-1, block.shape[-1])
    return result


class ChainSum:
    def __init__(self, links, order, keep, send):
        self.links, self.bits, self.terms = links, list(order[::-1]), [keep]
        self.pending = links.swap(send, links.core)

    def total(self, rows):
        return sum(term[rows].astype(F32) for term in self.terms)

    def prepare(self):
        self.terms.append(self.pending)
        near = self.pending.shape[0] // 2
        self.send = self.total(slice(near, 2 * near)).astype(LOW)
        self.terms = [term[:near] for term in self.terms]

    def launch(self):
        self.pending = self.links.swap(self.send, self.bits.pop(0))

    def result(self):
        self.terms.append(self.pending)
        return self.total(0)


class GroupSum:
    def __init__(self, links, flat):
        self.links = links
        self.chains = [
            ChainSum(links, order, flat[2 * chain], flat[2 * chain + 1])
            for chain, order in enumerate(links.orders)
        ]
        self.crossed = None

    def relay(self, value):
        if self.crossed is not None:
            return value
        if self.chains[0].bits:
            for chain in self.chains:
                chain.prepare()
            value, sends = lax.optimization_barrier((value, [chain.send for chain in self.chains]))
            for chain, send in zip(self.chains, sends):
                chain.send = send
                chain.launch()
            return value
        summed = [chain.result() for chain in self.chains]
        self.kept = jnp.concatenate([each[0] for each in summed], axis=1)
        send = jnp.concatenate([each[1].astype(LOW) for each in summed], axis=1)
        value, send = lax.optimization_barrier((value, send))
        self.crossed = self.links.swap(send, self.links.half)
        return value

    def finish(self):
        while self.crossed is None:
            self.relay(())
        return self.kept, self.crossed.astype(F32)


def pack_group(links, group, grads, rows):
    blocks = [grads[name].reshape(group.shape(name, links.count, rows)) for name in group.names]
    masks = [chain_masks(order) for order in links.orders]
    slots = len(masks[0])
    tables = [
        jnp.stack((links.owners(each), links.owners([mask ^ links.core for mask in each])))
        for each in masks
    ]
    if rows % 8 == 0:
        outs = []
        for cols in group.chain_cols:
            outs += [jax.ShapeDtypeStruct((slots, 2, rows, cols), LOW)] * 2
        kernel = functools.partial(pack_kernel, group, slots)
        flat = block_call(kernel, (jnp.stack(tables).reshape(-1),) + tuple(blocks), outs, "pack")
    else:
        whole = []
        for name, block in zip(group.names, blocks):
            if name == "shrink":
                block = block.transpose(0, 2, 1, 3).reshape(links.count, rows, -1)
            whole.append(block)
        whole = jnp.concatenate(whole, axis=2)
        flat = []
        for (start, stop), table in zip(group.bounds, tables):
            for which in range(2):
                taken = jnp.take(whole[:, :, start:stop], table[which].reshape(-1), axis=0)
                flat.append(taken.reshape((slots, 2) + taken.shape[1:]))
    return flat


def line_place(index, rows):
    per = LANES // rows
    return index // per, index % per * rows


def line_block(vectors, rows):
    block = jnp.zeros((rows, LANES), LOW)
    for index, vector in enumerate(vectors):
        row, lane = line_place(index, rows)
        spot = ((row, rows - row - 1), (lane, LANES - lane - rows))
        block = block + jnp.pad(vector.reshape(1, rows), spot)
    return block


def body(*args):
    tile_embeds, sentence_embeds, pairing = args[:3]
    visual_shards, textual_shards = args[3:16], args[16:27]
    sharpness_exponent, match_score_offset = args[27:]
    device = lax.axis_index(AXES)
    links = Links(lax.axis_size(AXES), device)
    count, half, low, side = links.count, links.half, links.low, links.side
    on_images = side == 0
    side_word = jnp.reshape(side, (1,)).astype(jnp.int32)
    micro, images, seq_len, width = tile_embeds.shape
    captions, text_len = sentence_embeds.shape[1:3]
    own_rows = micro * images * seq_len
    text_rows = micro * captions * text_len
    row_shards = visual_shards[2].shape[0]
    gather_groups = [Group(parts, width) for parts in GATHER_GROUPS]
    scatter_groups = [Group(parts, width) for parts in SCATTER_GROUPS]

    (v_gain_a, v_shift_a, v_triple, v_merge, v_gain_b, v_shift_b, v_expand, v_shrink) = (
        visual_shards[:8]
    )
    pool_gain, pool_shift, probe, keyval, pool_out = visual_shards[8:]
    (t_gain_a, t_shift_a, t_triple, t_merge, t_gain_b, t_shift_b, t_expand, t_shrink) = (
        textual_shards[:8]
    )
    final_gain, final_shift, readout = textual_shards[8:]
    visual_line = line_block(
        (v_gain_a, v_shift_a, v_gain_b, v_shift_b, pool_gain, pool_shift, probe), row_shards
    )
    textual_line = line_block(
        (t_gain_a, t_shift_a, t_gain_b, t_shift_b, final_gain, final_shift), row_shards
    )
    visual = dict(
        triple=v_triple,
        merge=v_merge,
        line=visual_line,
        expand=v_expand,
        keyval=keyval,
        head=pool_out,
        shrink=v_shrink,
    )
    textual = dict(
        triple=t_triple,
        merge=t_merge,
        line=textual_line,
        expand=t_expand,
        keyval=jnp.zeros_like(keyval),
        head=readout,
        shrink=t_shrink,
    )
    weights = {}
    collected = collect(side_word, gather_groups, visual, textual, row_shards)
    first = links.swap(collected[0][CHAINS], half)
    patch_rows = tile_embeds.reshape(own_rows, width)
    token_rows = jnp.pad(
        sentence_embeds.reshape(text_rows, width), ((0, own_rows - text_rows), (0, 0))
    )
    kept_rows = jnp.where(on_images, patch_rows, token_rows)
    moved_rows = jnp.where(on_images, token_rows, patch_rows)
    first, later = lax.optimization_barrier((first, collected[1][CHAINS]))
    later = links.swap(later, half)
    pieces = gather_pieces(links, gather_groups[0], collected[0][:CHAINS], first)
    across = [got[1] for got, _ in pieces]
    across, moved_rows, later = lax.optimization_barrier((across, moved_rows, later))
    for (got, _), far in zip(pieces, across):
        got[1] = far
    moved_rows = links.swap(moved_rows, half)
    weights.update(place_pieces(links, gather_groups[0], pieces, row_shards))
    pieces = gather_pieces(links, gather_groups[1], collected[1][:CHAINS], later)
    weights.update(place_pieces(links, gather_groups[1], pieces, row_shards))

    triple, merge, expand = weights["triple"], weights["merge"], weights["expand"]
    pool_keyval, head_matrix, shrink = weights["keyval"], weights["head"], weights["shrink"]
    per = LANES // row_shards
    line_rows = -(-7 // per)
    lines = weights["line"][:, :line_rows, : per * row_shards]
    lines = jnp.transpose(lines.reshape(count, line_rows, per, row_shards), (1, 2, 0, 3))
    vectors = lines.reshape(line_rows * per, width).astype(F32)
    gain_a, shift_a, gain_b, shift_b, gain_c, shift_c, probe_line = [vectors[k] for k in range(7)]

    shares = []
    for share in (kept_rows, moved_rows):
        share = share.astype(F32)
        hat_a, inverse_a = normalize_rows(share)
        normed_a = (hat_a * gain_a + shift_a).astype(LOW)
        triples = dot(normed_a, triple, 1, 0).astype(LOW)
        mixed = attend(side_word, triples, seq_len, text_len)
        shares.append((share, hat_a, inverse_a, normed_a, triples, mixed))
    inputs = jnp.concatenate([share[0] for share in shares], axis=0)
    mixed = jnp.concatenate([share[5] for share in shares], axis=0)
    middle = inputs + dot(mixed, merge, 1, 0)
    hat_b, inverse_b = normalize_rows(middle)
    normed_b = (hat_b * gain_b + shift_b).astype(LOW)
    upward = dot(normed_b, expand, 1, 0)
    active, slope = gelu_tanh(upward).astype(LOW), gelu_slope(upward).astype(LOW)
    active, slope = lax.optimization_barrier((active, slope))
    hidden = middle + dot(active, shrink, 1, 0)

    total_rows = 2 * own_rows
    group_count = total_rows // seq_len
    caption_slots = total_rows // text_len
    heads = width // HD
    hat_c, inverse_c = normalize_rows(hidden)
    normed_c = (hat_c * gain_c + shift_c).astype(LOW)
    pairs = dot(normed_c, pool_keyval, 1, 0).astype(LOW)
    keys, values = pairs[:, :width], pairs[:, width:]
    lane = lax.broadcasted_iota(jnp.int32, (width, 128), 0) // HD
    spread = lane == lax.broadcasted_iota(jnp.int32, (width, 128), 1)
    probe_map = jnp.where(spread, probe_line[:, None], 0.0).astype(LOW)
    spread_low = spread.astype(LOW)
    scores = (dot(keys, probe_map, 1, 0) * SCALE).reshape(group_count, seq_len, 128)
    row_exp = jnp.exp(scores - jnp.max(scores, axis=1, keepdims=True))
    pool_full = row_exp / jnp.sum(row_exp, axis=1, keepdims=True)
    pool_probs = pool_full.astype(LOW).reshape(total_rows, 128)
    probs_wide = dot(pool_probs, spread_low, 1, 1)
    pooled = jnp.sum((probs_wide * values).reshape(group_count, seq_len, width), axis=1)
    pooled = jnp.pad(pooled.astype(LOW), ((0, caption_slots - group_count), (0, 0)))
    last_rows = normed_c.reshape(caption_slots, text_len, width)[:, -1]
    head_in = jnp.where(on_images, pooled, last_rows)
    raw = dot(head_in, head_matrix, 1, 0)
    length_inverse = lax.rsqrt(jnp.sum(raw * raw, axis=-1, keepdims=True) + 1e-06)
    unit = raw * length_inverse

    their_unit = links.swap(unit, half)
    caption_half = caption_slots // 2
    own_texts = micro * captions
    image_units = jnp.where(on_images, unit, their_unit)[:IMAGE_ROWS]
    text_units = jnp.where(on_images, their_unit, unit)
    held = jnp.concatenate((image_units, text_units), axis=0).astype(LOW)[None]
    exchange = links.orders[0] + [links.core]
    for bit in exchange:
        held = jnp.concatenate((held, links.swap(held, bit)), axis=0)
    slot_rows = IMAGE_ROWS + caption_slots
    row = np.arange(slot_rows)
    is_image, text_row = row < group_count, row - IMAGE_ROWS
    in_half = text_row % caption_half
    is_text = (text_row >= 0) & (in_half < own_texts)
    place = np.where(is_image, row % (micro * images), in_half)
    pack = np.where(is_image, images, captions)
    row_side = np.where(is_image, row // (micro * images), 1 - text_row // caption_half)
    row_micro, row_item = np.where(is_image | is_text, place // pack, 0), place % pack
    slot_device = jnp.array(chain_masks(exchange), jnp.int32) ^ low
    row_device = slot_device[:, None] + jnp.array(row_side * half, jnp.int32)[None, :]
    all_images, all_captions = count * images, count * captions
    number = row_device * jnp.array(pack, jnp.int32)[None, :] + jnp.array(row_item, jnp.int32)
    number = jnp.where(jnp.array(is_image | is_text), number, 0)
    wanted = jnp.take(
        pairing.reshape(-1),
        jnp.where(jnp.array(is_text), number + jnp.array(row_micro * all_captions, jnp.int32), 0),
    )
    named = jnp.where(jnp.array(is_text), wanted, number)
    named = named + jnp.array(row_micro * all_images, jnp.int32)

    sharpness_factor = jnp.exp(sharpness_exponent[0])
    kind = np.where(is_image, 1, np.where(is_text, 2, 0)) + 4 * row_micro
    slots = slot_device.shape[0]

    def pair_terms(left, right, left_rows, right_rows, left_slots):
        left_kind = jnp.array(np.tile(kind[left_rows], left_slots))
        right_kind = jnp.array(np.tile(kind[right_rows], slots))
        together = (left_kind[:, None] + right_kind[None, :]) % 8 == 3
        together = jnp.logical_and(together, (left_kind[:, None] // 4) == (right_kind[None, :] // 4))
        matched = named[:left_slots, left_rows].reshape(-1)[:, None] == (
            named[:, right_rows].reshape(-1)[None, :]
        )
        signs = jnp.where(matched, 1.0, -1.0)
        cosine = dot(left, right, 1, 1)
        logits = sharpness_factor * cosine + match_score_offset[0]
        terms = jnp.where(together, jax.nn.softplus(-signs * logits), 0.0)
        grad_logits = jnp.where(together, -signs * jax.nn.sigmoid(-signs * logits), 0.0)
        return cosine, grad_logits, terms

    every_row, image_part, text_part = slice(None), slice(0, IMAGE_ROWS), slice(IMAGE_ROWS, None)
    flat = held.reshape(-1, width)
    _, grad_logits, _ = pair_terms(held[0], flat, every_row, every_row, 1)
    grad_cosine = (sharpness_factor * grad_logits).astype(LOW)
    own_grad = dot(grad_cosine, flat, 1, 0)
    from_texts = jnp.pad(own_grad[:IMAGE_ROWS], ((0, caption_slots - IMAGE_ROWS), (0, 0)))
    grad_unit = jnp.where(on_images, from_texts, own_grad[IMAGE_ROWS:])
    cosine, grad_logits, terms = pair_terms(
        held[:, image_part].reshape(-1, width),
        held[:, text_part].reshape(-1, width),
        image_part,
        text_part,
        slots,
    )
    objective = jnp.sum(terms)
    sharpness_grad = jnp.sum(grad_logits * cosine) * sharpness_factor
    offset_grad = jnp.sum(grad_logits)

    grad_raw = length_inverse * (grad_unit - unit * jnp.sum(grad_unit * unit, axis=-1, keepdims=True))
    grad_raw = grad_raw.astype(LOW)
    grad_head = dot(head_in, grad_raw, 0, 0).astype(LOW)
    grad_head_in = dot(grad_raw, head_matrix, 1, 1)
    grad_pooled = grad_head_in[:group_count].astype(LOW)
    pooled_wide = jnp.broadcast_to(grad_pooled[:, None], (group_count, seq_len, width))
    pooled_wide = pooled_wide.reshape(total_rows, width)
    grad_values = probs_wide * pooled_wide
    pooled_map = jnp.where(spread[None], grad_pooled[:, :, None], 0.0).astype(LOW)
    grad_probs = lax.dot_general(
        values.reshape(group_count, seq_len, width),
        pooled_map,
        (((2,), (1,)), ((0,), (0,))),
        preferred_element_type=F32,
    )
    delta = jnp.sum(grad_probs * pool_full, axis=1, keepdims=True)
    grad_scores = (pool_full * (grad_probs - delta)).astype(LOW).reshape(total_rows, 128)
    grad_keys = dot(grad_scores, probe_map, 1, 1) * SCALE
    grad_probe = jnp.sum(jnp.where(spread, dot(keys, grad_scores, 0, 0), 0.0), axis=1) * SCALE
    grad_pairs = jnp.concatenate((grad_keys.astype(LOW), grad_values.astype(LOW)), axis=1)
    grad_keyval = dot(normed_c, grad_pairs, 0, 0).astype(LOW)
    pool_side = dot(grad_pairs, pool_keyval, 1, 1)
    text_side = jnp.pad(grad_head_in[:, None], ((0, 0), (text_len - 1, 0), (0, 0)))
    grad_normed_c = jnp.where(on_images, pool_side, text_side.reshape(total_rows, width))
    grad_gain_c = jnp.sum(grad_normed_c * hat_c, axis=0)
    grad_shift_c = jnp.sum(grad_normed_c, axis=0)
    grad_hidden = normalize_back(grad_normed_c * gain_c, hat_c, inverse_c)

    grad_low = grad_hidden.astype(LOW)
    grad_shrink = dot(active, grad_low, 0, 0).astype(LOW)
    grads = dict(shrink=grad_shrink, keyval=grad_keyval, head=grad_head)
    packed = [pack_group(links, scatter_groups[0], grads, row_shards)]
    grad_up = (dot(grad_low, shrink, 1, 1) * slope.astype(F32)).astype(LOW)
    grad_up, packed = lax.optimization_barrier((grad_up, packed))
    sums = [GroupSum(links, packed[0])]
    grad_normed_b = dot(grad_up, expand, 1, 1)
    grad_gain_b = jnp.sum(grad_normed_b * hat_b, axis=0)
    grad_shift_b = jnp.sum(grad_normed_b, axis=0)
    grad_middle = grad_hidden + normalize_back(grad_normed_b * gain_b, hat_b, inverse_b)
    grad_branch, grad_up = sums[0].relay((grad_middle.astype(LOW), grad_up))
    grad_expand = dot(normed_b, grad_up, 0, 0).astype(LOW)
    grad_merge = dot(mixed, grad_branch, 0, 0).astype(LOW)
    grad_mixed = dot(grad_branch, merge, 1, 1).astype(LOW)
    grads = dict(merge=grad_merge, expand=grad_expand)
    packed = pack_group(links, scatter_groups[1], grads, row_shards)
    grad_mixed, packed = lax.optimization_barrier((grad_mixed, packed))
    sums.append(GroupSum(links, packed))
    grad_mixed = sums[0].relay(grad_mixed)

    def inputs_back(index, grad_triples):
        _, hat_a, inverse_a, _, _, _ = shares[index]
        grad_normed_a = dot(grad_triples, triple, 1, 1)
        grad_gain = jnp.sum(grad_normed_a * hat_a, axis=0)
        grad_shift = jnp.sum(grad_normed_a, axis=0)
        own = grad_middle[index * own_rows : (index + 1) * own_rows]
        return grad_gain, grad_shift, own + normalize_back(grad_normed_a * gain_a, hat_a, inverse_a)

    blocks = own_rows // seq_len
    moved_back = attend_back(side_word, shares[1][4], grad_mixed, blocks, seq_len, text_len)
    moved_back = sums[0].relay(moved_back)
    moved_back = sums[1].relay(moved_back)
    moved_gain, moved_shift, moved_grad = inputs_back(1, moved_back)
    moved_grad = moved_grad.astype(LOW)
    grad_mixed, moved_grad = lax.optimization_barrier((grad_mixed, moved_grad))
    returned = links.swap(moved_grad, half).astype(F32)
    kept_back = attend_back(side_word, shares[0][4], grad_mixed, 0, seq_len, text_len)
    kept_back = sums[1].relay(kept_back)
    kept_gain, kept_shift, kept = inputs_back(0, kept_back)
    grad_gain_a, grad_shift_a = kept_gain + moved_gain, kept_shift + moved_shift
    grad_triple = dot(shares[1][3], moved_back, 0, 0) + dot(shares[0][3], kept_back, 0, 0)
    grad_triple = sums[1].relay(grad_triple.astype(LOW))
    grad_triple = sums[0].relay(grad_triple)

    grad_lines = jnp.stack(
        (grad_gain_a, grad_shift_a, grad_gain_b, grad_shift_b, grad_gain_c, grad_shift_c, grad_probe)
    )
    grad_lines = jnp.pad(grad_lines, ((0, line_rows * per - 7), (0, 0)))
    grad_lines = jnp.transpose(
        grad_lines.reshape(line_rows, per, count, row_shards), (2, 0, 1, 3)
    ).reshape(count, line_rows, per * row_shards)
    grad_lines = jnp.pad(
        grad_lines.astype(LOW),
        ((0, 0), (0, row_shards - line_rows), (0, LANES - per * row_shards)),
    )
    grads = dict(triple=grad_triple, line=grad_lines)
    sums.append(GroupSum(links, pack_group(links, scatter_groups[2], grads, row_shards)))
    visual_sums, textual_sums = {}, {}
    for group, partial in zip(scatter_groups, sums):
        own_sum, crossed = partial.finish()
        for target, mine in ((visual_sums, on_images), (textual_sums, jnp.logical_not(on_images))):
            for name, quarter, at, cols in group.places:
                piece = jnp.where(mine, own_sum[:, at : at + cols], crossed[:, at : at + cols])
                target.setdefault(name, []).append(piece)

    def outputs_of(sums, names):
        line = sums["line"][0]
        vec = []
        for index in range(7):
            spot_row, lane = line_place(index, row_shards)
            vec.append(line[spot_row, lane : lane + row_shards])
        layer = (vec[0], vec[1], sums["triple"][0], sums["merge"][0], vec[2], vec[3])
        layer += (sums["expand"][0], jnp.concatenate(sums["shrink"], axis=0), vec[4], vec[5])
        if names == 0:
            return layer + (vec[6], sums["keyval"][0], sums["head"][0])
        return layer + (sums["head"][0],)

    patches_grad = jnp.where(on_images, kept, returned).reshape(tile_embeds.shape)
    captions_grad = jnp.where(on_images, returned[:text_rows], kept[:text_rows])
    own_group = group_count // 2
    image_embedding = jnp.where(on_images, unit[:own_group], their_unit[own_group:group_count])
    text_embedding = jnp.where(
        on_images, their_unit[caption_half : caption_half + own_texts], unit[:own_texts]
    )
    return (
        image_embedding.reshape(micro, images, width),
        text_embedding.reshape(micro, captions, width),
        objective / (micro * all_images),
        patches_grad,
        captions_grad.reshape(sentence_embeds.shape),
        *outputs_of(visual_sums, 0),
        *outputs_of(textual_sums, 1),
        jnp.reshape(sharpness_grad, (1,)),
        jnp.reshape(offset_grad, (1,)),
    )


def solution(mesh):
    row, matrix, batch, rest = P(AXES), P(AXES, None), P(None, AXES, None, None), P()
    layer = (row, row, matrix, matrix, row, row, matrix, matrix)
    visual = layer + (row, row, row, matrix, matrix)
    textual = layer + (row, row, matrix)
    in_specs = (batch, batch, rest) + visual + textual + (rest, rest)
    embed = P(None, AXES, None)
    out_specs = (embed, embed, rest, batch, batch) + visual + textual + (rest, rest)
    return jax.shard_map(body, mesh=mesh, in_specs=in_specs, out_specs=out_specs, check_vma=False)
```

```python
import functools

import jax
import jax.numpy as jnp
import numpy as np
from jax import lax
from jax.experimental import pallas as pl
from jax.experimental.pallas import tpu as pltpu
from jax.sharding import PartitionSpec as P

HD = 64
AXES = ("dp", "fsdp")
GELU_COEF = 0.7978845608028654
GELU_CUBE = 0.044715
F32 = jnp.float32
LOW = jnp.bfloat16
SCALE = HD ** (-0.5)

LANES = 128
CHAINS = 3
GATHER_GROUPS = (
    (("triple", 3), ("merge", 1), ("line", 0)),
    (("expand", 4), ("keyval", 2), ("head", 1), ("shrink", 4)),
)
SCATTER_GROUPS = (
    (("head", 1), ("keyval", 2), ("shrink", 4)),
    (("expand", 4), ("merge", 1)),
    (("triple", 3), ("line", 0)),
)
IMAGE_ROWS = 8


def dot(left, right, left_dim, right_dim):
    return lax.dot_general(
        left, right, (((left_dim,), (right_dim,)), ((), ())), preferred_element_type=F32
    )


def normalize_rows(values):
    centred = values - jnp.mean(values, axis=-1, keepdims=True)
    inverse = lax.rsqrt(jnp.mean(centred * centred, axis=-1, keepdims=True) + 1e-06)
    return (centred * inverse, inverse)


def normalize_back(grad_hat, hat_rows, inverse):
    first = jnp.mean(grad_hat, axis=-1, keepdims=True)
    second = jnp.mean(grad_hat * hat_rows, axis=-1, keepdims=True)
    return inverse * (grad_hat - first - hat_rows * second)


def gelu_parts(values):
    square = values * values
    inner = values * (GELU_COEF + (GELU_COEF * GELU_CUBE) * square)
    share = 0.5 + 0.5 * jnp.tanh(inner)
    active = values * share
    rise = 2.0 * GELU_COEF + (6.0 * GELU_COEF * GELU_CUBE) * square
    return active, share + active * (1.0 - share) * rise


def pair_bias(side_ref, seq_len, group):
    key = lax.broadcasted_iota(jnp.int32, (seq_len, seq_len), 0)
    query = lax.broadcasted_iota(jnp.int32, (seq_len, seq_len), 1)
    seen = jnp.logical_and(key // group == query // group, query >= key)
    seen = jnp.logical_or(seen, side_ref[0] == 0)
    return jnp.where(seen, 0.0, -1e30)

def head_lanes(shape):
    lane = lax.broadcasted_iota(jnp.int32, shape, 1)
    return (lane < HD, lane >= HD)

def head_probs(key, query_part, bias):
    scores = dot(key, query_part, 1, 1) + bias
    row_exp = jnp.exp(scores - jnp.max(scores, axis=0, keepdims=True))
    return row_exp * (1.0 / jnp.sum(row_exp, axis=0, keepdims=True))

def attend_kernel(group, side_ref, q_ref, k_ref, v_ref, out_ref, bias_ref):
    @pl.when(pl.program_id(0) == 0)
    def _():
        bias_ref[...] = pair_bias(side_ref, q_ref.shape[0], group)
    bias = bias_ref[...]
    pairs = q_ref.shape[1] // (2 * HD)
    def scores_of(pair):
        lanes = slice(pair * 2 * HD, (pair + 1) * 2 * HD)
        query, key = q_ref[:, lanes] * jnp.asarray(SCALE, LOW), k_ref[:, lanes]
        zero = jnp.zeros_like(query)
        return [dot(key, jnp.where(mine, query, zero), 1, 1) for mine in head_lanes(query.shape)]
    def finish(pair, scores):
        lanes = slice(pair * 2 * HD, (pair + 1) * 2 * HD)
        value_t = v_ref[:, lanes].T
        parts = []
        for head in range(2):
            masked = scores[head] + bias
            row_exp = jnp.exp(masked - jnp.max(masked, axis=0, keepdims=True))
            inverse = 1.0 / jnp.sum(row_exp, axis=0, keepdims=True)
            part = dot(value_t[head * HD : (head + 1) * HD], row_exp.astype(LOW), 1, 0)
            parts.append(part * inverse)
        out_ref[:, lanes] = jnp.concatenate(parts, axis=0).T.astype(LOW)
    for pair in range(pairs):
        finish(pair, scores_of(pair))

def attend_back_kernel(group, width, side_ref, q_ref, k_ref, v_ref, grad_ref, out_ref, bias_ref):
    @pl.when(pl.program_id(0) == 0)
    def _():
        bias_ref[...] = pair_bias(side_ref, q_ref.shape[0], group)
    bias = bias_ref[...]
    for pair in range(width // (2 * HD)):
        lanes = slice(pair * 2 * HD, (pair + 1) * 2 * HD)
        query, key, value = q_ref[:, lanes] * jnp.asarray(SCALE, LOW), k_ref[:, lanes], v_ref[:, lanes]
        grad = grad_ref[:, lanes]
        key_t = key.T
        zero = jnp.zeros_like(query)
        sides = head_lanes(query.shape)
        grad_q, grad_k, grad_v = [], [], []
        for head, mine in enumerate(sides):
            probs = head_probs(key, jnp.where(mine, query, zero), bias)
            grad_probs = dot(value, jnp.where(mine, grad, zero), 1, 1)
            delta = jnp.sum(grad_probs * probs, axis=0, keepdims=True)
            grad_scores = (probs * (grad_probs - delta)).astype(LOW)
            grad_q.append(dot(key_t[head * HD : (head + 1) * HD], grad_scores, 1, 0))
            grad_k.append(dot(grad_scores, query, 1, 0))
            grad_v.append(dot(probs.astype(LOW), grad, 1, 0))
        parts = (
            jnp.concatenate(grad_q, axis=0).T * SCALE,
            jnp.where(sides[0], grad_k[0], grad_k[1]),
            jnp.where(sides[0], grad_v[0], grad_v[1]),
        )
        for place, part in enumerate(parts):
            start = place * width + pair * 2 * HD
            out_ref[:, start : start + 2 * HD] = part.astype(LOW)

def triple_specs(seq_len, width):
    return [pl.BlockSpec((seq_len, width), lambda b, s, place=place: (b, place)) for place in range(3)]


def attend(side, triples, seq_len, group):
    rows, wide = triples.shape
    width = wide // 3
    return pl.pallas_call(
        functools.partial(attend_kernel, group),
        out_shape=jax.ShapeDtypeStruct((rows, width), LOW),
        grid_spec=pltpu.PrefetchScalarGridSpec(
            num_scalar_prefetch=1,
            grid=(rows // seq_len,),
            in_specs=triple_specs(seq_len, width),
            out_specs=pl.BlockSpec((seq_len, width), lambda b, s: (b, 0)),
            scratch_shapes=[pltpu.VMEM((seq_len, seq_len), F32)],
        ),
        cost_estimate=pl.CostEstimate(
            flops=4 * rows * seq_len * width,
            bytes_accessed=8 * rows * width,
            transcendentals=rows * seq_len * width // HD,
        ),
        name="attend",
    )(side, triples, triples, triples)


def attend_back(side, triples, grad_mixed, first, seq_len, group):
    rows, wide = triples.shape
    width = wide // 3
    return pl.pallas_call(
        functools.partial(attend_back_kernel, group, width),
        out_shape=jax.ShapeDtypeStruct((rows, wide), LOW),
        grid_spec=pltpu.PrefetchScalarGridSpec(
            num_scalar_prefetch=1,
            grid=(rows // seq_len,),
            in_specs=triple_specs(seq_len, width)
            + [pl.BlockSpec((seq_len, width), lambda b, s: (b + first, 0))],
            out_specs=pl.BlockSpec((seq_len, wide), lambda b, s: (b, 0)),
            scratch_shapes=[pltpu.VMEM((seq_len, seq_len), F32)],
        ),
        cost_estimate=pl.CostEstimate(
            flops=10 * rows * seq_len * width,
            bytes_accessed=14 * rows * width,
            transcendentals=rows * seq_len * width // HD,
        ),
        name="attend_back",
    )(side, triples, triples, triples, grad_mixed)


class Segment:
    def __init__(self, name, quarter, weight_col, chain, chain_col, cols):
        self.name, self.quarter, self.weight_col = name, quarter, weight_col
        self.chain, self.chain_col, self.cols = chain, chain_col, cols


class Group:
    def __init__(self, parts, width):
        self.names = [name for name, _ in parts]
        self.cols = {name: max(many * width, LANES) for name, many in parts}
        total = sum(self.cols.values())
        tiles = total // LANES
        cuts = [tiles * chain // CHAINS * LANES for chain in range(CHAINS + 1)]
        self.total = total
        self.bounds = list(zip(cuts[:-1], cuts[1:]))
        self.chain_cols = [stop - start for start, stop in self.bounds]
        self.segments, self.places = [], []
        at = 0
        for name, _ in parts:
            quarters = range(4) if name == "shrink" else (None,)
            cols = self.cols[name] // len(quarters)
            for quarter in quarters:
                self.places.append((name, quarter, at, cols))
                for chain, (start, stop) in enumerate(self.bounds):
                    low, high = max(at, start), min(at + cols, stop)
                    if low < high:
                        self.segments.append(
                            Segment(name, quarter, low - at, chain, low - start, high - low)
                        )
                at += cols

    def shape(self, name, count, rows):
        if name == "shrink":
            return (count, 4, rows, self.cols[name] // 4)
        return (count, rows, self.cols[name])


def window(ref, lead, quarter, col, cols):
    lead = lead if quarter is None else lead + (quarter,)
    return ref.at[lead + (slice(None), pl.ds(col, cols))]


def wait_whole(refs, sems):
    for place, ref in enumerate(refs):
        pltpu.make_async_copy(ref, ref, sems.at[place]).wait()


def block_call(kernel, operands, outs, name):
    anywhere = pl.BlockSpec(memory_space=pl.ANY)
    size = sum(2 * out.size * out.dtype.itemsize for out in outs)
    return pl.pallas_call(
        kernel,
        out_shape=outs,
        grid_spec=pltpu.PrefetchScalarGridSpec(
            num_scalar_prefetch=1,
            grid=(1,),
            in_specs=[anywhere] * (len(operands) - 1),
            out_specs=[pl.BlockSpec(memory_space=pltpu.VMEM)] * len(outs),
            scratch_shapes=[pltpu.SemaphoreType.DMA((len(outs),))],
        ),
        cost_estimate=pl.CostEstimate(flops=0, bytes_accessed=size, transcendentals=0),
        name=name,
    )(*operands)


def collect_kernel(groups, towers, side_ref, *refs):
    tower_refs = (refs[: len(towers[0])], refs[len(towers[0]) : len(towers[0]) + len(towers[1])])
    outs, sems = refs[len(towers[0]) + len(towers[1]) : -1], refs[-1]

    def fill(kept):
        for index, group in enumerate(groups):
            base = index * (CHAINS + 1)
            sources = dict(zip(towers[kept], tower_refs[kept]))
            for part in group.segments:
                if part.name in sources:
                    source = sources[part.name]
                    rows = outs[base].shape[0]
                    first = 0 if part.quarter is None else part.quarter * rows
                    pltpu.make_async_copy(
                        source.at[pl.ds(first, rows), pl.ds(part.weight_col, part.cols)],
                        outs[base + part.chain].at[:, pl.ds(part.chain_col, part.cols)],
                        sems.at[base + part.chain],
                    ).start()
            sources = dict(zip(towers[1 - kept], tower_refs[1 - kept]))
            for name, quarter, at, cols in group.places:
                if name in sources:
                    source = sources[name]
                    rows = outs[base].shape[0]
                    first = 0 if quarter is None else quarter * rows
                    pltpu.make_async_copy(
                        source.at[pl.ds(first, rows), :],
                        outs[base + CHAINS].at[:, pl.ds(at, cols)],
                        sems.at[base + CHAINS],
                    ).start()

    pl.when(side_ref[0] == 0)(lambda: fill(0))
    pl.when(side_ref[0] != 0)(lambda: fill(1))
    wait_whole(outs, sems)


def collect(side_word, groups, visual, textual, rows):
    outs = []
    for group in groups:
        outs += [jax.ShapeDtypeStruct((rows, cols), LOW) for cols in group.chain_cols]
        outs.append(jax.ShapeDtypeStruct((rows, group.total), LOW))
    if rows % 8 == 0:
        towers = (tuple(visual), tuple(textual))
        operands = (side_word,) + tuple(visual.values()) + tuple(textual.values())
        kernel = functools.partial(collect_kernel, groups, towers)
        flat = block_call(kernel, operands, outs, "collect")
    else:
        flat = []
        for group in groups:
            blocks = []
            for tower in (visual, textual):
                parts = []
                for name, quarter, _, cols in group.places:
                    first = 0 if quarter is None else quarter * rows
                    parts.append(tower[name][first : first + rows])
                blocks.append(jnp.concatenate(parts, axis=1))
            on_images = side_word[0] == 0
            mine = jnp.where(on_images, blocks[0], blocks[1])
            flat += [mine[:, start:stop] for start, stop in group.bounds]
            flat.append(jnp.where(on_images, blocks[1], blocks[0]))
    size = CHAINS + 1
    return [flat[k * size : (k + 1) * size] for k in range(len(groups))]


def spread_kernel(group, sizes, table_ref, *refs):
    pieces = refs[: sum(len(each) for each in sizes)]
    outs, sems = refs[len(pieces) : -1], refs[-1]
    place = {name: k for k, name in enumerate(group.names)}
    base, at = 0, 0
    for chain, each in enumerate(sizes):
        parts = [part for part in group.segments if part.chain == chain]
        for size in each:
            piece = pieces[at]
            at += 1

            def step(slot, carry, piece=piece, base=base, parts=parts):
                for j in range(2):
                    owner = table_ref[base + 2 * slot + j]
                    for part in parts:
                        target = place[part.name]
                        pltpu.make_async_copy(
                            window(piece, (slot, j), None, part.chain_col, part.cols),
                            window(outs[target], (owner,), part.quarter, part.weight_col, part.cols),
                            sems.at[target],
                        ).start()
                return carry

            lax.fori_loop(0, size, step, 0)
            base += 2 * size
    wait_whole(outs, sems)


def pack_kernel(group, slots, table_ref, *refs):
    grads, outs, sems = refs[: len(group.names)], refs[len(group.names) : -1], refs[-1]
    place = {name: k for k, name in enumerate(group.names)}
    for chain in range(CHAINS):
        parts = [part for part in group.segments if part.chain == chain]
        for which in range(2):
            base = (2 * chain + which) * 2 * slots
            target = 2 * chain + which

            def step(slot, carry, base=base, parts=parts, target=target):
                for j in range(2):
                    owner = table_ref[base + 2 * slot + j]
                    for part in parts:
                        source = grads[place[part.name]]
                        pltpu.make_async_copy(
                            window(source, (owner,), part.quarter, part.weight_col, part.cols),
                            window(outs[target], (slot, j), None, part.chain_col, part.cols),
                            sems.at[target],
                        ).start()
                return carry

            lax.fori_loop(0, slots, step, 0)
    wait_whole(outs, sems)


class Links:
    def __init__(self, count, device):
        self.count = count
        self.half = count // 2
        self.core = 2
        self.device = device
        self.low, self.side = device % self.half, device // self.half
        bits = [1 << place for place in range(self.half.bit_length() - 1)]
        outer = [bit for bit in bits if bit != self.core]
        third = max(1, len(outer) // 3)
        self.orders = [outer[place:] + outer[:place] for place in (0, third, 2 * third)]

    def swap(self, value, mask):
        return lax.ppermute(value, AXES, [(place, place ^ mask) for place in range(self.count)])

    def owners(self, masks):
        low = jnp.array(masks, jnp.int32) ^ self.low
        sides = jnp.stack((self.side, 1 - self.side)).astype(jnp.int32)
        return low[:, None] + sides[None, :] * self.half


def chain_masks(order):
    masks = [0]
    for bit in order:
        masks = masks + [mask ^ bit for mask in masks]
    return masks


def gather_near(links, group, kept, arrived):
    chains = []
    for chain, (order, (start, stop)) in enumerate(zip(links.orders, group.bounds)):
        held = jnp.stack((kept[chain], arrived[:, start:stop]))[None]
        for bit in order[:-1]:
            held = jnp.concatenate((held, links.swap(held, bit)), axis=0)
        chains.append(held)
    return chains


def gather_far(links, near):
    chains = []
    for order, held in zip(links.orders, near):
        far = links.swap(held, order[-1])
        pieces = [held, far, links.swap(held, links.core), links.swap(far, links.core)]
        masks = chain_masks(order)
        chains.append((pieces, masks + [mask ^ links.core for mask in masks]))
    return chains


def place_pieces(links, group, chains, rows):
    pieces = [got for got, _ in chains]
    sizes = [[piece.shape[0] for piece in got] for got in pieces]
    tables = [links.owners(masks) for _, masks in chains]
    shapes = [group.shape(name, links.count, rows) for name in group.names]
    if rows % 8 == 0:
        operands = (jnp.stack(tables).reshape(-1),) + tuple(p for got in pieces for p in got)
        outs = [jax.ShapeDtypeStruct(shape, LOW) for shape in shapes]
        kernel = functools.partial(spread_kernel, group, sizes)
        whole = block_call(kernel, operands, outs, "spread")
    else:
        columns = []
        for got, table in zip(pieces, tables):
            order = jnp.argsort(table.reshape(-1))
            every = jnp.concatenate(got, axis=0)
            columns.append(jnp.take(every.reshape((-1,) + every.shape[2:]), order, axis=0))
        every = jnp.concatenate(columns, axis=2)
        whole, at = [], 0
        for name in group.names:
            cols = group.cols[name]
            block = every[:, :, at : at + cols]
            if name == "shrink":
                block = block.reshape(links.count, rows, 4, cols // 4).transpose(0, 2, 1, 3)
            whole.append(block)
            at += cols
    result = {}
    for name, block in zip(group.names, whole):
        result[name] = block if name == "line" else block.reshape(-1, block.shape[-1])
    return result


def far_kernel(counts, *refs):
    outs, at = refs[sum(counts) :], 0
    for out, many in zip(outs, counts):
        out[...] = sum(ref[...].astype(F32) for ref in refs[at : at + many]).astype(LOW)
        at += many


def own_kernel(counts, *refs):
    own, send = refs[sum(counts) :]
    at, col = 0, 0
    for many in counts:
        total = sum(ref[0].astype(F32) for ref in refs[at : at + many])
        cols = slice(col, col + total.shape[-1])
        own[:, cols] = total[0]
        send[:, cols] = total[1].astype(LOW)
        at, col = at + many, cols.stop


def sum_call(kernel, chains, slots, index, outs, name):
    terms = [term for chain in chains for term in chain]
    specs = [
        pl.BlockSpec((slots,) + term.shape[1:], lambda step: (index, 0, 0, 0)) for term in terms
    ]
    size = sum(2 * slots * term[0].size for term in terms) + sum(2 * out.size for out in outs)
    return pl.pallas_call(
        functools.partial(kernel, [len(chain) for chain in chains]),
        out_shape=outs,
        grid=(1,),
        in_specs=specs,
        out_specs=[pl.BlockSpec(out.shape, lambda step, n=len(out.shape): (0,) * n) for out in outs],
        cost_estimate=pl.CostEstimate(flops=size, bytes_accessed=size, transcendentals=0),
        name=name,
    )(*terms)


class GroupSum:
    def __init__(self, links, flat):
        self.links, self.crossed = links, None
        self.bits = [list(order[::-1]) for order in links.orders]
        self.chains = [[keep] for keep in flat[::2]]
        self.pending = [links.swap(send, links.core) for send in flat[1::2]]
        self.slots = flat[0].shape[0]

    def relay(self, value):
        if self.crossed is not None:
            return value
        for chain, arrived in zip(self.chains, self.pending):
            chain.append(arrived)
        rows = self.chains[0][0].shape[2]
        if self.slots > 1:
            self.slots //= 2
            near = self.slots
            if rows % 8 == 0:
                outs = [
                    jax.ShapeDtypeStruct((near,) + chain[0].shape[1:], LOW) for chain in self.chains
                ]
                sends = sum_call(far_kernel, self.chains, near, 1, outs, "far_sum")
            else:
                sends = [
                    sum(term[near : 2 * near].astype(F32) for term in chain).astype(LOW)
                    for chain in self.chains
                ]
            value, sends = lax.optimization_barrier((value, sends))
            self.pending = [
                self.links.swap(send, bits.pop(0)) for send, bits in zip(sends, self.bits)
            ]
            return value
        cols = sum(chain[0].shape[3] for chain in self.chains)
        if rows % 8 == 0:
            outs = [jax.ShapeDtypeStruct((rows, cols), kind) for kind in (F32, LOW)]
            self.kept, send = sum_call(own_kernel, self.chains, 1, 0, outs, "own_sum")
        else:
            summed = [sum(term[0].astype(F32) for term in chain) for chain in self.chains]
            self.kept = jnp.concatenate([each[0] for each in summed], axis=1)
            send = jnp.concatenate([each[1].astype(LOW) for each in summed], axis=1)
        value, send = lax.optimization_barrier((value, send))
        self.crossed = self.links.swap(send, self.links.half)
        return value

    def finish(self):
        while self.crossed is None:
            self.relay(())
        return self.kept, self.crossed.astype(F32)


def pack_group(links, group, grads, rows):
    blocks = [grads[name].reshape(group.shape(name, links.count, rows)) for name in group.names]
    masks = [chain_masks(order) for order in links.orders]
    slots = len(masks[0])
    tables = [
        jnp.stack((links.owners(each), links.owners([mask ^ links.core for mask in each])))
        for each in masks
    ]
    if rows % 8 == 0:
        outs = []
        for cols in group.chain_cols:
            outs += [jax.ShapeDtypeStruct((slots, 2, rows, cols), LOW)] * 2
        kernel = functools.partial(pack_kernel, group, slots)
        flat = block_call(kernel, (jnp.stack(tables).reshape(-1),) + tuple(blocks), outs, "pack")
    else:
        whole = []
        for name, block in zip(group.names, blocks):
            if name == "shrink":
                block = block.transpose(0, 2, 1, 3).reshape(links.count, rows, -1)
            whole.append(block)
        whole = jnp.concatenate(whole, axis=2)
        flat = []
        for (start, stop), table in zip(group.bounds, tables):
            for which in range(2):
                taken = jnp.take(whole[:, :, start:stop], table[which].reshape(-1), axis=0)
                flat.append(taken.reshape((slots, 2) + taken.shape[1:]))
    return flat


def line_place(index, rows):
    per = LANES // rows
    return index // per, index % per * rows


def line_block(vectors, rows):
    block = jnp.zeros((rows, LANES), LOW)
    for index, vector in enumerate(vectors):
        row, lane = line_place(index, rows)
        spot = ((row, rows - row - 1), (lane, LANES - lane - rows))
        block = block + jnp.pad(vector.reshape(1, rows), spot)
    return block


def body(*args):
    tile_embeds, sentence_embeds, pairing = args[:3]
    visual_shards, textual_shards = args[3:16], args[16:27]
    sharpness_exponent, match_score_offset = args[27:]
    device = lax.axis_index(AXES)
    links = Links(lax.axis_size(AXES), device)
    count, half, low, side = links.count, links.half, links.low, links.side
    on_images = side == 0
    side_word = jnp.reshape(side, (1,)).astype(jnp.int32)
    micro, images, seq_len, width = tile_embeds.shape
    captions, text_len = sentence_embeds.shape[1:3]
    own_rows = micro * images * seq_len
    text_rows = micro * captions * text_len
    row_shards = visual_shards[2].shape[0]
    gather_groups = [Group(parts, width) for parts in GATHER_GROUPS]
    scatter_groups = [Group(parts, width) for parts in SCATTER_GROUPS]

    (v_gain_a, v_shift_a, v_triple, v_merge, v_gain_b, v_shift_b, v_expand, v_shrink) = (
        visual_shards[:8]
    )
    pool_gain, pool_shift, probe, keyval, pool_out = visual_shards[8:]
    (t_gain_a, t_shift_a, t_triple, t_merge, t_gain_b, t_shift_b, t_expand, t_shrink) = (
        textual_shards[:8]
    )
    final_gain, final_shift, readout = textual_shards[8:]
    visual_line = line_block(
        (v_gain_a, v_shift_a, v_gain_b, v_shift_b, pool_gain, pool_shift, probe), row_shards
    )
    textual_line = line_block(
        (t_gain_a, t_shift_a, t_gain_b, t_shift_b, final_gain, final_shift), row_shards
    )
    visual = dict(
        triple=v_triple,
        merge=v_merge,
        line=visual_line,
        expand=v_expand,
        keyval=keyval,
        head=pool_out,
        shrink=v_shrink,
    )
    textual = dict(
        triple=t_triple,
        merge=t_merge,
        line=textual_line,
        expand=t_expand,
        keyval=jnp.zeros_like(keyval),
        head=readout,
        shrink=t_shrink,
    )
    weights = {}
    collected = collect(side_word, gather_groups, visual, textual, row_shards)
    first = links.swap(collected[0][CHAINS], half)
    patch_rows = tile_embeds.reshape(own_rows, width)
    token_rows = jnp.pad(
        sentence_embeds.reshape(text_rows, width), ((0, own_rows - text_rows), (0, 0))
    )
    kept_rows = jnp.where(on_images, patch_rows, token_rows)
    moved_rows = jnp.where(on_images, token_rows, patch_rows)
    first, moved_rows = lax.optimization_barrier((first, moved_rows))
    moved_rows = links.swap(moved_rows, half)
    near = gather_near(links, gather_groups[0], collected[0][:CHAINS], first)
    near, later = lax.optimization_barrier((near, collected[1][CHAINS]))
    later = links.swap(later, half)
    pieces = gather_far(links, near)
    across = [got[1] for got, _ in pieces]
    across, later = lax.optimization_barrier((across, later))
    for (got, _), far in zip(pieces, across):
        got[1] = far
    weights.update(place_pieces(links, gather_groups[0], pieces, row_shards))
    near = gather_near(links, gather_groups[1], collected[1][:CHAINS], later)

    triple, merge = weights["triple"], weights["merge"]
    per = LANES // row_shards
    line_rows = -(-7 // per)
    lines = weights["line"][:, :line_rows, : per * row_shards]
    lines = jnp.transpose(lines.reshape(count, line_rows, per, row_shards), (1, 2, 0, 3))
    vectors = lines.reshape(line_rows * per, width).astype(F32)
    gain_a, shift_a, gain_b, shift_b, gain_c, shift_c, probe_line = [vectors[k] for k in range(7)]

    shares = []
    for share in (kept_rows, moved_rows):
        if shares:
            share, _ = lax.optimization_barrier((share, shares[0][5]))
        share = share.astype(F32)
        hat_a, inverse_a = normalize_rows(share)
        normed_a = (hat_a * gain_a + shift_a).astype(LOW)
        triples = dot(normed_a, triple, 1, 0).astype(LOW)
        if not shares:
            triples, near = lax.optimization_barrier((triples, near))
            pieces = gather_far(links, near)
        mixed = attend(side_word, triples, seq_len, text_len)
        shares.append((share, hat_a, inverse_a, normed_a, triples, mixed))
    weights.update(place_pieces(links, gather_groups[1], pieces, row_shards))
    expand, shrink = weights["expand"], weights["shrink"]
    pool_keyval, head_matrix = weights["keyval"], weights["head"]
    inputs = jnp.concatenate([share[0] for share in shares], axis=0)
    mixed = jnp.concatenate([share[5] for share in shares], axis=0)
    middle = inputs + dot(mixed, merge, 1, 0)
    hat_b, inverse_b = normalize_rows(middle)
    normed_b = (hat_b * gain_b + shift_b).astype(LOW)
    upward = dot(normed_b, expand, 1, 0)
    active, slope = gelu_parts(upward)
    active, slope = lax.optimization_barrier((active.astype(LOW), slope.astype(LOW)))
    hidden = middle + dot(active, shrink, 1, 0)

    total_rows = 2 * own_rows
    group_count = total_rows // seq_len
    caption_slots = total_rows // text_len
    heads = width // HD
    hat_c, inverse_c = normalize_rows(hidden)
    normed_c = (hat_c * gain_c + shift_c).astype(LOW)
    pairs = dot(normed_c, pool_keyval, 1, 0).astype(LOW)
    keys, values = pairs[:, :width], pairs[:, width:]
    lane = lax.broadcasted_iota(jnp.int32, (width, 128), 0) // HD
    spread = lane == lax.broadcasted_iota(jnp.int32, (width, 128), 1)
    probe_map = jnp.where(spread, probe_line[:, None], 0.0).astype(LOW)
    spread_low = spread.astype(LOW)
    scores = (dot(keys, probe_map, 1, 0) * SCALE).reshape(group_count, seq_len, 128)
    row_exp = jnp.exp(scores - jnp.max(scores, axis=1, keepdims=True))
    pool_full = row_exp / jnp.sum(row_exp, axis=1, keepdims=True)
    pool_probs = pool_full.astype(LOW).reshape(total_rows, 128)
    probs_wide = dot(pool_probs, spread_low, 1, 1)
    pooled = jnp.sum((probs_wide * values).reshape(group_count, seq_len, width), axis=1)
    pooled = jnp.pad(pooled.astype(LOW), ((0, caption_slots - group_count), (0, 0)))
    last_rows = normed_c.reshape(caption_slots, text_len, width)[:, -1]
    head_in = jnp.where(on_images, pooled, last_rows)
    raw = dot(head_in, head_matrix, 1, 0)
    length_inverse = lax.rsqrt(jnp.sum(raw * raw, axis=-1, keepdims=True) + 1e-06)
    unit = raw * length_inverse

    their_unit = links.swap(unit, half)
    caption_half = caption_slots // 2
    own_texts = micro * captions
    image_units = jnp.where(on_images, unit, their_unit)[:IMAGE_ROWS]
    text_units = jnp.where(on_images, their_unit, unit)
    held = jnp.concatenate((image_units, text_units), axis=0).astype(LOW)[None]
    exchange = links.orders[0] + [links.core]
    for bit in exchange:
        held = jnp.concatenate((held, links.swap(held, bit)), axis=0)
    slot_rows = IMAGE_ROWS + caption_slots
    row = np.arange(slot_rows)
    is_image, text_row = row < group_count, row - IMAGE_ROWS
    in_half = text_row % caption_half
    is_text = (text_row >= 0) & (in_half < own_texts)
    place = np.where(is_image, row % (micro * images), in_half)
    pack = np.where(is_image, images, captions)
    row_side = np.where(is_image, row // (micro * images), 1 - text_row // caption_half)
    row_micro, row_item = np.where(is_image | is_text, place // pack, 0), place % pack
    slot_device = jnp.array(chain_masks(exchange), jnp.int32) ^ low
    row_device = slot_device[:, None] + jnp.array(row_side * half, jnp.int32)[None, :]
    all_images, all_captions = count * images, count * captions
    number = row_device * jnp.array(pack, jnp.int32)[None, :] + jnp.array(row_item, jnp.int32)
    number = jnp.where(jnp.array(is_image | is_text), number, 0)
    wanted = jnp.take(
        pairing.reshape(-1),
        jnp.where(jnp.array(is_text), number + jnp.array(row_micro * all_captions, jnp.int32), 0),
    )
    named = jnp.where(jnp.array(is_text), wanted, number)
    named = named + jnp.array(row_micro * all_images, jnp.int32)

    sharpness_factor = jnp.exp(sharpness_exponent[0])
    kind = np.where(is_image, 1, np.where(is_text, 2, 0)) + 4 * row_micro
    slots = slot_device.shape[0]

    def pair_terms(left, right, left_rows, right_rows, left_slots):
        left_kind = jnp.array(np.tile(kind[left_rows], left_slots))
        right_kind = jnp.array(np.tile(kind[right_rows], slots))
        together = (left_kind[:, None] + right_kind[None, :]) % 8 == 3
        together = jnp.logical_and(together, (left_kind[:, None] // 4) == (right_kind[None, :] // 4))
        matched = named[:left_slots, left_rows].reshape(-1)[:, None] == (
            named[:, right_rows].reshape(-1)[None, :]
        )
        signs = jnp.where(matched, 1.0, -1.0)
        cosine = dot(left, right, 1, 1)
        logits = sharpness_factor * cosine + match_score_offset[0]
        terms = jnp.where(together, jax.nn.softplus(-signs * logits), 0.0)
        grad_logits = jnp.where(together, -signs * jax.nn.sigmoid(-signs * logits), 0.0)
        return cosine, grad_logits, terms

    every_row, image_part, text_part = slice(None), slice(0, IMAGE_ROWS), slice(IMAGE_ROWS, None)
    flat = held.reshape(-1, width)
    _, grad_logits, _ = pair_terms(held[0], flat, every_row, every_row, 1)
    grad_cosine = (sharpness_factor * grad_logits).astype(LOW)
    own_grad = dot(grad_cosine, flat, 1, 0)
    from_texts = jnp.pad(own_grad[:IMAGE_ROWS], ((0, caption_slots - IMAGE_ROWS), (0, 0)))
    grad_unit = jnp.where(on_images, from_texts, own_grad[IMAGE_ROWS:])
    cosine, grad_logits, terms = pair_terms(
        held[:, image_part].reshape(-1, width),
        held[:, text_part].reshape(-1, width),
        image_part,
        text_part,
        slots,
    )
    objective = jnp.sum(terms)
    sharpness_grad = jnp.sum(grad_logits * cosine) * sharpness_factor
    offset_grad = jnp.sum(grad_logits)

    grad_raw = length_inverse * (grad_unit - unit * jnp.sum(grad_unit * unit, axis=-1, keepdims=True))
    grad_raw = grad_raw.astype(LOW)
    grad_head = dot(head_in, grad_raw, 0, 0).astype(LOW)
    grad_head_in = dot(grad_raw, head_matrix, 1, 1)
    grad_pooled = grad_head_in[:group_count].astype(LOW)
    pooled_wide = jnp.broadcast_to(grad_pooled[:, None], (group_count, seq_len, width))
    pooled_wide = pooled_wide.reshape(total_rows, width)
    grad_values = probs_wide * pooled_wide
    pooled_map = jnp.where(spread[None], grad_pooled[:, :, None], 0.0).astype(LOW)
    grad_probs = lax.dot_general(
        values.reshape(group_count, seq_len, width),
        pooled_map,
        (((2,), (1,)), ((0,), (0,))),
        preferred_element_type=F32,
    )
    delta = jnp.sum(grad_probs * pool_full, axis=1, keepdims=True)
    grad_scores = (pool_full * (grad_probs - delta)).astype(LOW).reshape(total_rows, 128)
    grad_keys = dot(grad_scores, probe_map, 1, 1) * SCALE
    grad_probe = jnp.sum(jnp.where(spread, dot(keys, grad_scores, 0, 0), 0.0), axis=1) * SCALE
    grad_pairs = jnp.concatenate((grad_keys.astype(LOW), grad_values.astype(LOW)), axis=1)
    grad_keyval = dot(normed_c, grad_pairs, 0, 0).astype(LOW)
    pool_side = dot(grad_pairs, pool_keyval, 1, 1)
    text_side = jnp.pad(grad_head_in[:, None], ((0, 0), (text_len - 1, 0), (0, 0)))
    grad_normed_c = jnp.where(on_images, pool_side, text_side.reshape(total_rows, width))
    grad_gain_c = jnp.sum(grad_normed_c * hat_c, axis=0)
    grad_shift_c = jnp.sum(grad_normed_c, axis=0)
    grad_hidden = normalize_back(grad_normed_c * gain_c, hat_c, inverse_c)

    grad_low = grad_hidden.astype(LOW)
    grad_shrink = dot(active, grad_low, 0, 0).astype(LOW)
    grads = dict(shrink=grad_shrink, keyval=grad_keyval, head=grad_head)
    packed = [pack_group(links, scatter_groups[0], grads, row_shards)]
    grad_up = (dot(grad_low, shrink, 1, 1) * slope.astype(F32)).astype(LOW)
    grad_up, packed = lax.optimization_barrier((grad_up, packed))
    sums = [GroupSum(links, packed[0])]
    grad_normed_b = dot(grad_up, expand, 1, 1)
    grad_gain_b = jnp.sum(grad_normed_b * hat_b, axis=0)
    grad_shift_b = jnp.sum(grad_normed_b, axis=0)
    grad_middle = grad_hidden + normalize_back(grad_normed_b * gain_b, hat_b, inverse_b)
    grad_branch, grad_up = sums[0].relay((grad_middle.astype(LOW), grad_up))
    grad_expand = dot(normed_b, grad_up, 0, 0).astype(LOW)
    grad_branch, grad_expand = sums[0].relay((grad_branch, grad_expand))
    grad_merge = dot(mixed, grad_branch, 0, 0).astype(LOW)
    grad_mixed = dot(grad_branch, merge, 1, 1).astype(LOW)
    grads = dict(merge=grad_merge, expand=grad_expand)
    packed = pack_group(links, scatter_groups[1], grads, row_shards)
    grad_mixed, packed = lax.optimization_barrier((grad_mixed, packed))
    sums.append(GroupSum(links, packed))

    def inputs_back(index, grad_triples):
        _, hat_a, inverse_a, _, _, _ = shares[index]
        grad_normed_a = dot(grad_triples, triple, 1, 1)
        grad_gain = jnp.sum(grad_normed_a * hat_a, axis=0)
        grad_shift = jnp.sum(grad_normed_a, axis=0)
        own = grad_middle[index * own_rows : (index + 1) * own_rows]
        return grad_gain, grad_shift, own + normalize_back(grad_normed_a * gain_a, hat_a, inverse_a)

    blocks = own_rows // seq_len
    moved_back = attend_back(side_word, shares[1][4], grad_mixed, blocks, seq_len, text_len)
    moved_back = sums[0].relay(moved_back)
    moved_back = sums[1].relay(moved_back)
    moved_gain, moved_shift, moved_grad = inputs_back(1, moved_back)
    moved_grad = moved_grad.astype(LOW)
    grad_mixed, moved_grad = lax.optimization_barrier((grad_mixed, moved_grad))
    returned = links.swap(moved_grad, half).astype(F32)
    kept_back = attend_back(side_word, shares[0][4], grad_mixed, 0, seq_len, text_len)
    kept_back = sums[1].relay(kept_back)
    kept_gain, kept_shift, kept = inputs_back(0, kept_back)
    grad_gain_a, grad_shift_a = kept_gain + moved_gain, kept_shift + moved_shift
    grad_triple = dot(shares[1][3], moved_back, 0, 0) + dot(shares[0][3], kept_back, 0, 0)
    grad_triple = grad_triple.astype(LOW)

    grad_lines = jnp.stack(
        (grad_gain_a, grad_shift_a, grad_gain_b, grad_shift_b, grad_gain_c, grad_shift_c, grad_probe)
    )
    grad_lines = jnp.pad(grad_lines, ((0, line_rows * per - 7), (0, 0)))
    grad_lines = jnp.transpose(
        grad_lines.reshape(line_rows, per, count, row_shards), (2, 0, 1, 3)
    ).reshape(count, line_rows, per * row_shards)
    grad_lines = jnp.pad(
        grad_lines.astype(LOW),
        ((0, 0), (0, row_shards - line_rows), (0, LANES - per * row_shards)),
    )
    grads = dict(triple=grad_triple, line=grad_lines)
    packed = pack_group(links, scatter_groups[2], grads, row_shards)
    sums.append(GroupSum(links, packed))
    first, second, third = sums
    first.pending, second.pending = third.relay((first.pending, second.pending))
    third.pending = first.relay(third.pending)
    third.pending = second.relay(third.pending)
    second.pending = third.relay(second.pending)
    third.pending = second.relay(third.pending)
    visual_sums, textual_sums = {}, {}
    for group, partial in zip(scatter_groups, sums):
        own_sum, crossed = partial.finish()
        for target, mine in ((visual_sums, on_images), (textual_sums, jnp.logical_not(on_images))):
            for name, quarter, at, cols in group.places:
                piece = jnp.where(mine, own_sum[:, at : at + cols], crossed[:, at : at + cols])
                target.setdefault(name, []).append(piece)

    def outputs_of(sums, names):
        line = sums["line"][0]
        vec = []
        for index in range(7):
            spot_row, lane = line_place(index, row_shards)
            vec.append(line[spot_row, lane : lane + row_shards])
        layer = (vec[0], vec[1], sums["triple"][0], sums["merge"][0], vec[2], vec[3])
        layer += (sums["expand"][0], jnp.concatenate(sums["shrink"], axis=0), vec[4], vec[5])
        if names == 0:
            return layer + (vec[6], sums["keyval"][0], sums["head"][0])
        return layer + (sums["head"][0],)

    patches_grad = jnp.where(on_images, kept, returned).reshape(tile_embeds.shape)
    captions_grad = jnp.where(on_images, returned[:text_rows], kept[:text_rows])
    own_group = group_count // 2
    image_embedding = jnp.where(on_images, unit[:own_group], their_unit[own_group:group_count])
    text_embedding = jnp.where(
        on_images, their_unit[caption_half : caption_half + own_texts], unit[:own_texts]
    )
    return (
        image_embedding.reshape(micro, images, width),
        text_embedding.reshape(micro, captions, width),
        objective / (micro * all_images),
        patches_grad,
        captions_grad.reshape(sentence_embeds.shape),
        *outputs_of(visual_sums, 0),
        *outputs_of(textual_sums, 1),
        jnp.reshape(sharpness_grad, (1,)),
        jnp.reshape(offset_grad, (1,)),
    )


def solution(mesh):
    row, matrix, batch, rest = P(AXES), P(AXES, None), P(None, AXES, None, None), P()
    layer = (row, row, matrix, matrix, row, row, matrix, matrix)
    visual = layer + (row, row, row, matrix, matrix)
    textual = layer + (row, row, matrix)
    in_specs = (batch, batch, rest) + visual + textual + (rest, rest)
    embed = P(None, AXES, None)
    out_specs = (embed, embed, rest, batch, batch) + visual + textual + (rest, rest)
    return jax.shard_map(body, mesh=mesh, in_specs=in_specs, out_specs=out_specs, check_vma=False)
```
